128 devices in a mesh: box: 4 (over y), samp: 32 (over x, z, core).
Axes of the slice: x: 4, y: 4, z: 4, core: 2. Of those that a mesh axis runs over, the one named last changes fastest.
Arguments:
- density: bfloat16 [2048, 2, 128], P(('box', 'samp')), may hold values from -6 to 6
- radiate: bfloat16 [2048, 128, 1024], P(('box', 'samp')), may hold values from -0.5 to 0.5
- receive: bfloat16 [2048, 128, 1024], P(('box', 'samp')), may hold values from -0.1875 to 0.1875
- near_tiles: bfloat16 [28672, 2, 128, 128], P(('box', 'samp')), may hold values from -0.109375 to 0.109375
- near_src: int32 [2048, 27], P(('box', 'samp')), may hold values from 0 to 2048, as said below
- near_tile: int32 [2048, 27], P(('box', 'samp')), may hold values from 0 to 28672, as said below
- send_box: int32 [128, 128, 4], P(('box', 'samp')), may hold values from 0 to 16, as said below
- distant_pattern_slot: int32 [2048, 189], P(('box', 'samp')), may hold values from 0 to 512, as said below
- far_type: int32 [2048, 189], P(('box', 'samp')), may hold values from 0 to 315
- trans_lo: bfloat16 [316, 2, 512], replicated, may hold values from -0.4375 to 0.4375
- interp_matrix: bfloat16 [512, 2048], replicated, may hold values from -0.25 to 0.25
- shifts: float32 [8, 2, 2048], replicated, may hold values from -2 to 2
- par_far: int32 [256, 189], P('box'), may hold values from 0 to 256, as said below
- par_type: int32 [256, 189], P('box'), may hold values from 0 to 315
- trans_hi: bfloat16 [316, 2, 2048], replicated, may hold values from -0.4375 to 0.4375
Outputs:
- field: float32 [2048, 2, 128], P(('box', 'samp'))
The draws below stay inside these ranges and needn't reach their ends.
Inputs may be any that keep to these rules, and one draw needn't show every extreme that they name: `send_box`: entries equal to 16 are empty and come last in a slot row. A sender fills slots for a receiver only if it lies within 8 device numbers of it, or is 64, 32 or 16 device numbers away cyclically; for every other pair all slots are empty. One device sends 4 patterns to another in every draw, and some device receives 4 from every device that fills slots for it. `distant_pattern_slot`: the value 128 * 4 marks an empty entry; empty entries come last in a row; every other entry names a non-empty slot that its sender fills for the box's device; at least 94 entries of a row are non-empty. `near_src`: the value 2048 marks an empty entry; empty entries come last in a row; a source box lies on the box's own device or on the device of index one lower or one higher. `near_tile`: empty where near_src is; every other entry names a tile of the box's own device, and the non-empty entries of one device's boxes name each of its 224 tiles once. `par_far`: the value 256 marks an empty entry; empty entries come last in a row; at least 94 entries of a row are non-empty.
All inputs are finite; a program needn't handle non-finite values.
Results may differ from the reference program's by a relative error of at most 0.0065.
Values may be sent and summed in bfloat16 or wider, within the bound.
A program may use at most 128 MiB of HBM per device.

```python
import jax
import jax.numpy as jnp
from jax import lax

BOX_DEV = 16
PANELS = 128
Q_LO = 512
Q_HI = 2048
NEAR = 27
FAR = 189
TYPES = 316
SLOTS = 4
REACH = 8
NDEV = 128
NBOX = 2048
NPAR = 256
TILE_DEV = 224


def jump_table():
    return jnp.array([NDEV // 2, NDEV // 4, NDEV - NDEV // 4, NDEV // 8, NDEV - NDEV // 8], jnp.int32)


def linked_pairs():
    emitter_values = jnp.arange(NDEV)[:, None]
    destination = jnp.arange(NDEV)[None, :]
    apart = (emitter_values - destination) % NDEV
    nearby = jnp.abs(emitter_values - destination) <= REACH
    jumps = jump_table()
    across = jnp.any(apart[:, :, None] == jumps[None, None, :], 2)
    return nearby | across


def slot_counts(key):
    base = jax.random.fold_in(key, 7001)
    tally_per_kind = jax.random.randint(jax.random.fold_in(base, 1), (NDEV, NDEV), 1, SLOTS + 1)
    target = jax.random.randint(jax.random.fold_in(base, 3), (), 0, NDEV)
    emitter_values = jnp.arange(NDEV)[:, None]
    destination = jnp.arange(NDEV)[None, :]
    linked = linked_pairs()
    filled = ((emitter_values - destination) % NDEV == NDEV // 2) | (destination == target)
    return jnp.where(linked, jnp.where(filled, SLOTS, tally_per_kind), 0)


def draw_send_box(key, part):
    tally_per_kind = slot_counts(key)
    chosen = jax.random.randint(jax.random.fold_in(key, 7101), (NDEV, NDEV, SLOTS), 0, BOX_DEV)
    position = jnp.arange(SLOTS)[None, None, :]
    return jnp.where(position < tally_per_kind[:, :, None], chosen, BOX_DEV).astype(jnp.int32)


def draw_distant_pattern_slot(key, part):
    tally_per_kind = slot_counts(key)
    receiver = (jnp.arange(NBOX) // BOX_DEV)[:, None]
    half_reach = REACH // 2
    step_one = jax.random.randint(jax.random.fold_in(key, 7204), (NBOX, FAR), -half_reach, half_reach + 1)
    step_two = jax.random.randint(jax.random.fold_in(key, 7205), (NBOX, FAR), -half_reach, half_reach + 1)
    local_sender = jnp.clip(receiver + step_one + step_two, 0, NDEV - 1)
    jump_index = jax.random.randint(jax.random.fold_in(key, 7206), (NBOX, FAR), 0, 5)
    far_sender = (receiver + jump_table()[jump_index]) % NDEV
    crossing = jax.random.randint(jax.random.fold_in(key, 7207), (NBOX, FAR), 0, 4) == 0
    sender = jnp.where(crossing, far_sender, local_sender)
    limits = tally_per_kind[sender, receiver]
    within = jax.random.randint(jax.random.fold_in(key, 7202), (NBOX, FAR), 0, limits)
    live_count = jax.random.randint(jax.random.fold_in(key, 7203), (NBOX, 1), FAR // 2, FAR + 1)
    column = jnp.arange(FAR)[None, :]
    return jnp.where(column < live_count, sender * SLOTS + within, NDEV * SLOTS).astype(jnp.int32)


def permuted(subkey):
    return jax.random.permutation(subkey, TILE_DEV)


def near_layout(key):
    base = jax.random.fold_in(key, 7301)
    half_count = (NEAR + 1) // 2
    spread = jax.random.randint(jax.random.fold_in(base, 1), (NDEV, BOX_DEV // 2), -(NEAR // 2), NEAR // 2 + 1)
    fullest = jax.random.randint(jax.random.fold_in(base, 2), (), 0, NDEV)
    spread = spread.at[fullest, 0].set(NEAR // 2)
    tally_per_kind = jnp.stack([half_count + spread, half_count - spread], 2).reshape(NDEV, BOX_DEV)
    starts = jnp.cumsum(tally_per_kind, 1) - tally_per_kind
    orders = jax.vmap(permuted)(jax.random.split(jax.random.fold_in(base, 3), NDEV))
    column = jnp.arange(NEAR)
    position = starts[:, :, None] + column[None, None, :]
    live = column[None, None, :] < tally_per_kind[:, :, None]
    safe_position = jnp.minimum(position, TILE_DEV - 1).reshape(NDEV, BOX_DEV * NEAR)
    picked = jnp.take_along_axis(orders, safe_position, 1).reshape(NDEV, BOX_DEV, NEAR)
    owner = jnp.arange(NDEV)[:, None, None]
    tiles = jnp.where(live, owner * TILE_DEV + picked, NDEV * TILE_DEV)
    step_side = jax.random.randint(jax.random.fold_in(base, 4), (NDEV, BOX_DEV, NEAR), -1, 2)
    neighbour = jnp.clip(owner + step_side, 0, NDEV - 1)
    local_box = jax.random.randint(jax.random.fold_in(base, 5), (NDEV, BOX_DEV, NEAR), 0, BOX_DEV)
    sources = jnp.where(live, neighbour * BOX_DEV + local_box, NBOX)
    return (sources.reshape(NBOX, NEAR).astype(jnp.int32), tiles.reshape(NBOX, NEAR).astype(jnp.int32))


def draw_near_src(key, part):
    return near_layout(key)[0]


def draw_near_tile(key, part):
    return near_layout(key)[1]


def draw_par_far(key, part):
    chosen = jax.random.randint(jax.random.fold_in(key, 7401), (NPAR, FAR), 0, NPAR)
    live_count = jax.random.randint(jax.random.fold_in(key, 7402), (NPAR, 1), FAR // 2, FAR + 1)
    column = jnp.arange(FAR)[None, :]
    return jnp.where(column < live_count, chosen, NPAR).astype(jnp.int32)


def plant(values, own_key, least, largest):
    extent = values.shape
    index_at = [jax.random.randint(jax.random.fold_in(own_key, axis), (), 0, extent[axis]) for axis in range(len(extent))]
    values = values.at[tuple(index_at)].set(least)
    longest = extent.index(max(extent))
    index_at[longest] = (index_at[longest] + 1) % extent[longest]
    return values.at[tuple(index_at)].set(largest)


def block_levels(rng, shape, pieces, least, high):
    level = 1.0
    for dim, blocks in pieces:
        steps = jax.random.uniform(jax.random.fold_in(jax.random.fold_in(rng, 6), dim), (blocks,), jnp.float32, least / len(pieces), high / len(pieces))
        level = level * jnp.repeat(jnp.exp(steps), shape[dim] // blocks).reshape((-1,) + (1,) * (len(shape) - 1 - dim))
    return level


def noise(stream_key, shape, scale, bound, pieces=(), held_as=jnp.bfloat16):
    drawn = scale * jax.random.normal(stream_key, shape, jnp.float32)
    if pieces:
        drawn = drawn * block_levels(stream_key, shape, pieces, -0.22, 0.18)
    return jnp.clip(drawn, -bound, bound).astype(held_as)


def setup_inputs(seed: int = 0) -> dict:
    arg_keys = jax.random.split(jax.random.key(seed), 16)
    density = noise(arg_keys[0], (NBOX, 2, PANELS), 1.0, 6.0, ((0, 128),))
    radiate = noise(arg_keys[1], (NBOX, PANELS, 2 * Q_LO), PANELS ** -0.5, 0.5, ((0, 128),))
    receive = noise(arg_keys[2], (NBOX, PANELS, 2 * Q_LO), (2 * Q_LO) ** -0.5, 0.1875, ((0, 128),))
    near_tiles = noise(arg_keys[3], (NBOX * ((NEAR + 1) // 2), 2, PANELS, PANELS), (PANELS * NEAR) ** -0.5, 0.109375, ((0, 128),))
    near_src = draw_near_src(jax.random.fold_in(arg_keys[15], 71), 0)
    near_tile = draw_near_tile(jax.random.fold_in(arg_keys[15], 71), 0)
    send_box = draw_send_box(jax.random.fold_in(arg_keys[15], 71), 0)
    distant_pattern_slot = draw_distant_pattern_slot(jax.random.fold_in(arg_keys[15], 71), 0)
    far_type = plant(jax.random.randint(arg_keys[8], (NBOX, FAR), 0, TYPES), jax.random.fold_in(arg_keys[8], 1), 0, TYPES - 1).astype(jnp.int32)
    trans_lo = noise(arg_keys[9], (TYPES, 2, Q_LO), FAR ** -0.5, 0.4375)
    interp_matrix = noise(arg_keys[10], (Q_LO, Q_HI), Q_LO ** -0.5, 0.25)
    shifts = noise(arg_keys[11], (8, 2, Q_HI), 8 ** -0.5, 2.0, (), jnp.float32)
    par_far = draw_par_far(jax.random.fold_in(arg_keys[15], 71), 0)
    par_type = plant(jax.random.randint(arg_keys[13], (NPAR, FAR), 0, TYPES), jax.random.fold_in(arg_keys[13], 1), 0, TYPES - 1).astype(jnp.int32)
    trans_hi = noise(arg_keys[14], (TYPES, 2, Q_HI), FAR ** -0.5, 0.4375)
    return {"density": density, "radiate": radiate, "receive": receive, "near_tiles": near_tiles, "near_src": near_src, "near_tile": near_tile, "send_box": send_box, "distant_pattern_slot": distant_pattern_slot, "far_type": far_type, "trans_lo": trans_lo, "interp_matrix": interp_matrix, "shifts": shifts, "par_far": par_far, "par_type": par_type, "trans_hi": trans_hi}


def radiated(density, radiate):
    half_width = radiate.shape[-1] // 2
    matvec_result = jnp.einsum("lmq,lqj->lmj", density.astype(jnp.float32), radiate.astype(jnp.float32))
    real_part = matvec_result[:, 0, :half_width] - matvec_result[:, 1, half_width:]
    imag_part = matvec_result[:, 0, half_width:] + matvec_result[:, 1, :half_width]
    return jnp.stack([real_part, imag_part], 1)


def translated(pattern_in, operator_in):
    emitter_values = pattern_in.astype(jnp.float32)
    factor = operator_in.astype(jnp.float32)
    real_part = jnp.sum(factor[..., 0, :] * emitter_values[..., 0, :] - factor[..., 1, :] * emitter_values[..., 1, :], -2)
    imag_part = jnp.sum(factor[..., 0, :] * emitter_values[..., 1, :] + factor[..., 1, :] * emitter_values[..., 0, :], -2)
    return jnp.stack([real_part, imag_part], -2)


def shifted_sum(interpolated, shifts):
    width = interpolated.shape[-1]
    grouped = interpolated.reshape(-1, 8, 2, width)
    real_part = jnp.sum(grouped[:, :, 0] * shifts[:, 0] - grouped[:, :, 1] * shifts[:, 1], 1)
    imag_part = jnp.sum(grouped[:, :, 0] * shifts[:, 1] + grouped[:, :, 1] * shifts[:, 0], 1)
    return jnp.stack([real_part, imag_part], 1)


def spread_down(incoming_hi, shifts):
    parent = incoming_hi[:, None]
    real_part = shifts[None, :, 0] * parent[:, :, 0] + shifts[None, :, 1] * parent[:, :, 1]
    imag_part = shifts[None, :, 0] * parent[:, :, 1] - shifts[None, :, 1] * parent[:, :, 0]
    stacked = jnp.stack([real_part, imag_part], 2)
    return stacked.reshape(-1, 2, incoming_hi.shape[-1]).astype(jnp.bfloat16)


def received_field(receive, incoming):
    real_in = incoming[:, 0]
    imag_in = incoming[:, 1]
    blending_operator = jnp.stack([jnp.concatenate([real_in, -imag_in], -1), jnp.concatenate([imag_in, real_in], -1)], 1)
    return jnp.einsum("mws,mis->miw", receive.astype(jnp.float32), blending_operator.astype(jnp.float32))


def reference(density, radiate, receive, near_tiles, near_src, near_tile, send_box, distant_pattern_slot, far_type, trans_lo, interp_matrix, shifts, par_far, par_type, trans_hi):
    pattern_lo = radiated(density, radiate).astype(jnp.bfloat16)
    receiver = (jnp.arange(NBOX, dtype=jnp.int32) // BOX_DEV)[:, None]
    live = distant_pattern_slot < NDEV * SLOTS
    sender = jnp.minimum(distant_pattern_slot // SLOTS, NDEV - 1)
    within = distant_pattern_slot % SLOTS
    chosen = send_box[sender, receiver, within]
    far_source = jnp.where(live, sender * BOX_DEV + chosen, NBOX).astype(jnp.int32)
    padded_lo = jnp.concatenate([pattern_lo, jnp.zeros((1, 2, Q_LO), jnp.bfloat16)], 0)

    def far_box(entries):
        rows, kinds = entries
        return translated(padded_lo[rows], trans_lo[kinds])

    incoming_lo = lax.map(far_box, (far_source, far_type))
    interpolated = jnp.einsum("gcq,qh->gch", pattern_lo.astype(jnp.float32), interp_matrix.astype(jnp.float32))
    pattern_hi = shifted_sum(interpolated, shifts).astype(jnp.bfloat16)
    padded_hi = jnp.concatenate([pattern_hi, jnp.zeros((1, 2, Q_HI), jnp.bfloat16)], 0)

    def far_parent(entries):
        rows, kinds = entries
        return translated(padded_hi[rows], trans_hi[kinds])

    incoming_hi = lax.map(far_parent, (par_far, par_type))
    down = spread_down(incoming_hi, shifts)
    from_parent = jnp.einsum("gch,qh->gcq", down.astype(jnp.float32), interp_matrix.astype(jnp.float32))
    incoming = (incoming_lo + from_parent).astype(jnp.bfloat16)
    far_field = received_field(receive, incoming)
    density_pad = jnp.concatenate([density, jnp.zeros((1, 2, PANELS), jnp.bfloat16)], 0)
    tiles_pad = jnp.concatenate([near_tiles, jnp.zeros((1, 2, PANELS, PANELS), jnp.bfloat16)], 0)

    def near_box(entries):
        sources, tiles = entries
        values = density_pad[sources].astype(jnp.float32)
        blocks = tiles_pad[tiles].astype(jnp.float32)
        matvec_result = jnp.einsum("naij,nbj->abi", blocks, values)
        return jnp.stack([matvec_result[0, 0] - matvec_result[1, 1], matvec_result[0, 1] + matvec_result[1, 0]], 0)

    close_range_field = lax.map(near_box, (near_src, near_tile))
    return 0.5 * density.astype(jnp.float32) + close_range_field + far_field
```

```python
import functools

import jax
import jax.numpy as jnp
from jax import lax
from jax.experimental import pallas as pl
from jax.experimental.pallas import tpu as pltpu
from jax.sharding import PartitionSpec as P

F32 = jnp.float32
BF16 = jnp.bfloat16
I32 = jnp.int32
JUMPS = (16, 32, 64, 96, 112)
TPAD = 384
GROUP = 16


def nn(a, b):
    return lax.dot_general(a, b, (((1,), (0,)), ((), ())), preferred_element_type=F32)


def nt(a, b):
    return lax.dot_general(a, b, (((1,), (1,)), ((), ())), preferred_element_type=F32)


def rows_of(shape):
    return lax.broadcasted_iota(I32, shape, 0)


def lanes_of(shape):
    return lax.broadcasted_iota(I32, shape, 1)


def onehot(mask):
    return jnp.where(mask, 1.0, 0.0).astype(BF16)


def device(pos):
    return (pos // 32, pos % 32)


def kernel(
    dens, sb, near_src, near_tile, dps_in, ftype_in, pfar_in, ptype_in, shift_rows,
    radiate, receive, tiles, interp, lo_rows, hi_rows,
    out,
    dens_f, win_f, nidx, dps, ftype, pfar, ptype, shifts, lo_v, lo_f, hi_v, hi_f, tlo, thi, pat3, lo_sem, hi_sem,
    rad_v, rec_v, tile_v, int_v, window, patf, leaf_msg, leaf_in, hi_scr, one_msg, one_in, one_f,
    two_msg, two_in, hi_p, ret_msg, ret_in, down, n_lo, w_lo, p_lo, n_hi, w_hi, inc_lo, contrib, picked,
    rad_sem, rec_sem, tile_sem, int_sem, loc_sem,
    win_s, win_r, leaf_s, leaf_r, one_s, one_r, two_s, two_r, ret_s, ret_r,
):
    y = lax.axis_index("box")
    s = lax.axis_index("samp")
    me = y * 32 + s
    zc = s % 8
    yx = y * 4 + s // 8

    def rad_copy(i):
        sl = pl.ds(i * 256, 256)
        return pltpu.make_async_copy(radiate.at[sl], rad_v.at[sl], rad_sem.at[i])

    def rec_copy(i):
        sl = pl.ds(i * 256, 256)
        return pltpu.make_async_copy(receive.at[sl], rec_v.at[sl], rec_sem.at[i])

    def tile_copy(i):
        sl = pl.ds(i * GROUP, GROUP)
        return pltpu.make_async_copy(tiles.at[sl], tile_v.at[sl], tile_sem.at[i])

    int_copy = pltpu.make_async_copy(interp, int_v, int_sem)
    groups = tiles.shape[0] // GROUP

    lo_copy = pltpu.make_async_copy(lo_rows, lo_v, lo_sem)
    hi_copy = pltpu.make_async_copy(hi_rows.at[:, pl.ds((zc // 4) * 16, 16), :], hi_v, hi_sem)

    for i in range(8):
        rad_copy(i).start()
    int_copy.start()
    lo_copy.start()
    hi_copy.start()

    barrier = pltpu.get_barrier_semaphore()

    @pl.loop(1, 16)
    def _(i):
        pl.semaphore_signal(barrier, inc=1, device_id=device((me + 8 * i) % 128), device_id_type=pl.DeviceIdType.MESH)

    @pl.loop(1, 8)
    def _(i):
        pl.semaphore_signal(barrier, inc=1, device_id=device((me + i) % 128), device_id_type=pl.DeviceIdType.MESH)
        pl.semaphore_signal(barrier, inc=1, device_id=device((me + 128 - i) % 128), device_id_type=pl.DeviceIdType.MESH)

    @pl.loop(0, groups)
    def _(i):
        tile_copy(i).start()

    @pl.loop(0, 8)
    def _(i):
        rec_copy(i).start()

    def send(src, dst, ss, rs, pos):
        return pltpu.make_async_remote_copy(
            src_ref=src, dst_ref=dst, send_sem=ss, recv_sem=rs, device_id=device(pos), device_id_type=pl.DeviceIdType.MESH
        )

    dens_f[...] = dens[...].astype(F32)
    d_re = dens_f[pl.ds(0, 16, stride=2), :]
    d_im = dens_f[pl.ds(1, 16, stride=2), :]
    d_all = jnp.concatenate([d_re, d_im], 0)
    own = rows_of((32, 128)) % 16
    acc = jnp.zeros((32, 1024), F32)
    for i in range(8):
        rad_copy(i).wait()
        lhs = jnp.concatenate(
            [jnp.where(own == 2 * i + h, d_all, 0.0).astype(BF16) for h in range(2)], 1
        )
        acc = acc + nn(lhs, rad_v[i * 256 : (i + 1) * 256])
    pat = jnp.concatenate([acc[:16, :512] - acc[16:, 512:], acc[:16, 512:] + acc[16:, :512]], 0).astype(BF16)
    pat_f = pat.astype(F32)
    for m in range(2):
        for b in range(4):
            patf[pl.ds(m * 4 + b, 16, stride=8), :] = pat_f[m * 16 : (m + 1) * 16, b * 128 : (b + 1) * 128]
    pat3[...] = patf[...].reshape(16, 8, 128)
    for m in range(2):
        for b in range(16):
            shifts[m, :, b * 128 : (b + 1) * 128] = shift_rows[pl.ds(b * 2 + m, 8, stride=32), :]

    pl.semaphore_wait(barrier, 29)

    up_copy = send(dens, window.at[0], win_s.at[0], win_r.at[0], (me + 1) % 128)
    low_copy = send(dens, window.at[2], win_s.at[1], win_r.at[1], (me + 127) % 128)
    up_copy.start()
    low_copy.start()
    window[1] = dens[...]

    def fill(dst, j, receiver):
        for half in range(2):
            parts = []
            for k in range(2):
                box = jnp.minimum(sb[half * 2 + k, receiver], 15)
                parts.append(pat3[box])
            dst[j, pl.ds(half * 16, 16), :] = jnp.concatenate(parts, 0).astype(BF16)

    def near_send(j):
        return send(leaf_msg.at[j], leaf_in.at[16 - j], leaf_s.at[j], leaf_r.at[16 - j], (me + j + 120) % 128)

    def jump_send(i):
        return send(
            leaf_msg.at[17 + i], leaf_in.at[21 - i], leaf_s.at[17 + i], leaf_r.at[21 - i], (me + JUMPS[i]) % 128
        )

    int_copy.wait()
    up = nn(pat, int_v[...])
    s_re = shifts[0]
    s_im = shifts[1]
    for p in range(2):
        re = up[p * 8 : p * 8 + 8]
        im = up[16 + p * 8 : 24 + p * 8]
        vals = (
            jnp.sum(re * s_re - im * s_im, 0, keepdims=True),
            jnp.sum(re * s_im + im * s_re, 0, keepdims=True),
        )
        for m in range(2):
            for c in range(8):
                for h in range(2):
                    b = c * 2 + h
                    hi_scr[c, pl.ds(m * 4 + h * 2 + p, 1), :] = vals[m][:, b * 128 : (b + 1) * 128]
    one_msg[...] = hi_scr[...].astype(BF16)

    def one_send(i):
        peer = (zc + i) % 8
        return send(one_msg.at[peer], one_in.at[zc], one_s.at[i], one_r.at[i], yx * 8 + peer)

    @pl.loop(1, 8)
    def _(i):
        one_send(i).start()

    one_in[zc] = one_msg[zc]

    @pl.loop(0, 8)
    def _(j):
        fill(leaf_msg, j, (me + j + 120) % 128)
        near_send(j).start()

    @pl.loop(9, 17)
    def _(j):
        fill(leaf_msg, j, (me + j + 120) % 128)
        near_send(j).start()

    for i in range(5):
        fill(leaf_msg, 17 + i, (me + JUMPS[i]) % 128)
        jump_send(i).start()
    fill(leaf_in, 8, me)

    nidx[...] = jnp.full((8, 128), -1, I32)
    for g in range(16):
        at = (g % 4) * 32
        nidx[g // 4 : g // 4 + 1, at : at + 27] = near_src[g : g + 1, :]
        nidx[4 + g // 4 : 5 + g // 4, at : at + 27] = near_tile[g : g + 1, :]
    column = s // 8
    part = pl.ds(pl.multiple_of(column * 16, 16), 16)
    for held, given in ((dps, dps_in[...]), (ftype, ftype_in[...]), (pfar, pfar_in[part, :]), (ptype, ptype_in[part, :])):
        held[...] = jnp.full((16, 256), -1, I32)
        held[:, :189] = given
    lo_copy.wait()
    lo_f[:2528, :] = lo_v[...].astype(F32)
    lo_f[2528:, :] = jnp.zeros((544, 128), F32)
    for r in range(8):
        at = (r % 2) * 512 + (r // 2) * 128
        tlo[:, at : at + 128] = lo_f[pl.ds(r, TPAD, stride=8), :].astype(BF16)
    hi_copy.wait()

    @pl.loop(0, 4)
    def _(i):
        hi_f[pl.ds(pl.multiple_of(i * 1264, 16), 1264), :] = hi_v[pl.ds(i * 79, 79)].astype(F32).reshape(1264, 128)

    hi_f[5056:, :] = jnp.zeros((1088, 128), F32)
    for r in range(4):
        at = (r % 2) * 256 + (r // 2) * 128
        thi[:, at : at + 128] = hi_f[pl.ds((zc % 4) * 4 + r, TPAD, stride=16), :].astype(BF16)

    row = rows_of((96, 256))
    slot = row // 4
    delta = jnp.where(
        slot <= 16,
        slot - 8,
        jnp.where(slot == 17, 16, jnp.where(slot == 18, 32, jnp.where(slot == 19, 64, jnp.where(slot == 20, 96, 112)))),
    )
    expect = jnp.where(row < 88, ((me + delta + 128) % 128) * 4 + row % 4, -2)
    kinds = rows_of((TPAD, 256))

    @pl.loop(0, 16)
    def _(g):
        a = onehot(dps[pl.ds(g, 1), :] == expect)
        b = onehot(ftype[pl.ds(g, 1), :] == kinds)
        n_lo[pl.ds(pl.multiple_of(g * 96, 32), 96), :] = nt(a, b).astype(BF16)

    @pl.loop(1, 8)
    def _(i):
        one_send(i).wait_recv()

    one_f[...] = one_in[...].astype(F32).reshape(64, 128)
    for m in range(4):
        two_msg[m] = jnp.concatenate(
            [one_f[pl.ds(m * 2 + p, 8, stride=8), :] for p in range(2)], 0
        ).astype(BF16)

    def two_send(i):
        peer = (yx + i) % 16
        return send(two_msg, two_in.at[yx], two_s.at[i], two_r.at[i], peer * 8 + zc)

    @pl.loop(1, 16)
    def _(i):
        two_send(i).start()

    two_in[yx] = two_msg[...]

    @pl.loop(0, 4)
    def _(i):
        sl = pl.ds(pl.multiple_of(i * 384, 384), 384)
        w_lo[sl, :] = nn(n_lo[sl, :], tlo[...])

    prow = rows_of((256, 256))
    parent = (prow // 16) * 16 + (prow % 8) * 2 + (prow // 8) % 2

    @pl.loop(0, 16)
    def _(g):
        a = onehot(pfar[pl.ds(g, 1), :] == parent)
        b = onehot(ptype[pl.ds(g, 1), :] == kinds)
        n_hi[pl.ds(pl.multiple_of(g * 256, 256), 256), :] = nt(a, b).astype(BF16)

    @pl.loop(0, 8)
    def _(i):
        sl = pl.ds(pl.multiple_of(i * 512, 512), 512)
        w_hi[sl, :] = nn(n_hi[sl, :], thi[...])

    up_copy.wait_recv()
    low_copy.wait_recv()
    tile_rows = me * 224 + rows_of((224, 128))
    live = jnp.concatenate([onehot(nidx[pl.ds(4 + r, 1), :] == tile_rows) for r in range(4)], 1)
    box_rows = (me - 1) * 16 + rows_of((48, 128))
    source = jnp.concatenate([onehot(nidx[pl.ds(r, 1), :] == box_rows) for r in range(4)], 1)
    owner = jnp.concatenate(
        [onehot(rows_of((16, 128)) == 4 * r + lanes_of((16, 128)) // 32) for r in range(4)], 1
    )
    own_tile = nt(owner, live).astype(BF16)
    select = nt(live, source).astype(BF16)
    win_f[...] = window[...].astype(F32).reshape(96, 128)
    x_re = win_f[pl.ds(0, 48, stride=2), :]
    x_im = win_f[pl.ds(1, 48, stride=2), :]
    values = jnp.concatenate([x_re, -x_im, x_im, x_re], 1).astype(BF16)
    picked[...] = nn(select, values).astype(BF16)

    @pl.loop(0, groups)
    def _(grp):
        tile_copy(grp).wait()
        base = pl.multiple_of(grp * GROUP, GROUP)
        x = picked[pl.ds(base, GROUP), :]
        lhs = jnp.concatenate([x[:, :256], x[:, 256:]], 0)
        local = rows_of((2 * GROUP, 128)) % GROUP
        total = jnp.zeros((2 * GROUP, 128), F32)
        for q in range(GROUP // 2):
            pair = []
            for u in range(2):
                t = base + 2 * q + u
                pair.append(jnp.concatenate([tile_v[t, 0], tile_v[t, 1]], 1))
            res = nt(lhs, jnp.concatenate(pair, 0))
            for u in range(2):
                total = total + jnp.where(local == 2 * q + u, res[:, u * 128 : (u + 1) * 128], 0.0)
        contrib[pl.ds(base, GROUP), :] = jnp.concatenate([total[:GROUP], total[GROUP:]], 1)

    whole = contrib[...]
    high = whole.astype(BF16)
    near = nn(own_tile, high) + nn(own_tile, (whole - high.astype(F32)).astype(BF16))

    @pl.loop(1, 16)
    def _(i):
        two_send(i).wait_recv()

    for m in range(4):
        for i in range(16):
            hi_p[m, i * 16 : (i + 1) * 16, :] = two_in[i, m].astype(F32)

    @pl.loop(0, 8)
    def _(c):
        for p in range(2):
            base = pl.multiple_of((c * 2 + p) * 256, 256)
            for h in range(2):
                wr = w_hi[pl.ds(base, 256), h * 128 : (h + 1) * 128]
                wi = w_hi[pl.ds(base, 256), 256 + h * 128 : 256 + (h + 1) * 128]
                pr = hi_p[h]
                pi = hi_p[2 + h]
                ret_msg[c, pl.ds(h * 2 + p, 1), :] = jnp.sum(wr * pr - wi * pi, 0, keepdims=True)
                ret_msg[c, pl.ds(4 + h * 2 + p, 1), :] = jnp.sum(wr * pi + wi * pr, 0, keepdims=True)

    def ret_send(i):
        peer = (zc + i) % 8
        return send(ret_msg.at[peer], ret_in.at[zc], ret_s.at[i], ret_r.at[i], yx * 8 + peer)

    @pl.loop(1, 8)
    def _(i):
        ret_send(i).start()

    ret_in[zc] = ret_msg[zc]

    @pl.loop(0, 8)
    def _(j):
        near_send(j).wait_recv()

    @pl.loop(9, 17)
    def _(j):
        near_send(j).wait_recv()

    for i in range(5):
        jump_send(i).wait_recv()

    p_lo[...] = leaf_in[...].astype(F32).reshape(704, 128)

    @pl.loop(0, 16)
    def _(g):
        base = pl.multiple_of(g * 96, 32)
        reals, imags = [], []
        for b in range(4):
            wr = w_lo[pl.ds(base, 88), b * 128 : (b + 1) * 128]
            wi = w_lo[pl.ds(base, 88), 512 + b * 128 : 512 + (b + 1) * 128]
            pr = p_lo[pl.ds(b, 88, stride=8), :]
            pi = p_lo[pl.ds(4 + b, 88, stride=8), :]
            reals.append(jnp.sum(wr * pr - wi * pi, 0, keepdims=True))
            imags.append(jnp.sum(wr * pi + wi * pr, 0, keepdims=True))
        inc_lo[pl.ds(pl.multiple_of(g * 8, 8), 8), :] = jnp.concatenate(reals + imags, 0)

    @pl.loop(1, 8)
    def _(i):
        ret_send(i).wait_recv()

    for c in range(8):
        for h in range(2):
            b = c * 2 + h
            sr = shifts[0, :, b * 128 : (b + 1) * 128]
            si = shifts[1, :, b * 128 : (b + 1) * 128]
            parts = ([], [])
            for p in range(2):
                ir = ret_in[c, pl.ds(h * 2 + p, 1), :]
                ii = ret_in[c, pl.ds(4 + h * 2 + p, 1), :]
                parts[0].append(sr * ir + si * ii)
                parts[1].append(sr * ii - si * ir)
            for m in range(2):
                down[m * 16 : (m + 1) * 16, b * 128 : (b + 1) * 128] = jnp.concatenate(parts[m], 0).astype(BF16)
    direct = jnp.concatenate(
        [
            jnp.concatenate([inc_lo[pl.ds(m * 4 + b, 16, stride=8), :] for b in range(4)], 1)
            for m in range(2)
        ],
        0,
    )
    incoming = (direct + nt(down[...], int_v[...])).astype(BF16)
    in_re = incoming[:16]
    in_im = incoming[16:]
    lhs = jnp.concatenate([jnp.concatenate([in_re, -in_im], 1), jnp.concatenate([in_im, in_re], 1)], 0)
    far = jnp.zeros((32, 128), F32)
    for i in range(8):
        rec_copy(i).wait()
        res = nt(lhs, rec_v[i * 256 : (i + 1) * 256])
        for u in range(2):
            far = far + jnp.where(own == 2 * i + u, res[:, u * 128 : (u + 1) * 128], 0.0)
    out[pl.ds(0, 16, stride=2), :] = 0.5 * d_re + near[:, :128] + far[:16]
    out[pl.ds(1, 16, stride=2), :] = 0.5 * d_im + near[:, 128:] + far[16:]

    up_copy.wait_send()
    low_copy.wait_send()

    @pl.loop(1, 8)
    def _(i):
        one_send(i).wait_send()
        ret_send(i).wait_send()

    @pl.loop(1, 16)
    def _(i):
        two_send(i).wait_send()

    @pl.loop(0, 8)
    def _(j):
        near_send(j).wait_send()

    @pl.loop(9, 17)
    def _(j):
        near_send(j).wait_send()

    for i in range(5):
        jump_send(i).wait_send()


def on_device(
    density, radiate, receive, near_tiles, near_src, near_tile, send_box, distant_pattern_slot, far_type,
    trans_lo, interp_matrix, shifts, par_far, par_type, trans_hi,
):
    types = trans_lo.shape[0]
    lo_rows = trans_lo.reshape(types, 2, 4, 128).transpose(0, 2, 1, 3).reshape(types * 8, 128)
    hi_rows = trans_hi.reshape(types, 2, 16, 128).transpose(0, 2, 1, 3).reshape(types, 32, 128)
    shift_rows = shifts.reshape(8, 2, 16, 128).transpose(0, 2, 1, 3).reshape(256, 128)

    vm = pl.BlockSpec(memory_space=pltpu.VMEM)
    anyspace = pl.BlockSpec(memory_space=pl.ANY)
    dma = pltpu.SemaphoreType.DMA
    res = pl.pallas_call(
        kernel,
        name="mlfmm",
        out_shape=jax.ShapeDtypeStruct((32, 128), F32),
        in_specs=[vm, pl.BlockSpec(memory_space=pltpu.SMEM)] + [vm] * 7 + [anyspace] * 6,
        out_specs=vm,
        scratch_shapes=[
            pltpu.VMEM((32, 128), F32),
            pltpu.VMEM((96, 128), F32),
            pltpu.VMEM((8, 128), I32),
            pltpu.VMEM((16, 256), I32),
            pltpu.VMEM((16, 256), I32),
            pltpu.VMEM((16, 256), I32),
            pltpu.VMEM((16, 256), I32),
            pltpu.VMEM((2, 8, 2048), F32),
            pltpu.VMEM((2528, 128), BF16),
            pltpu.VMEM((TPAD * 8, 128), F32),
            pltpu.VMEM((316, 16, 128), BF16),
            pltpu.VMEM((TPAD * 16, 128), F32),
            pltpu.VMEM((TPAD, 1024), BF16),
            pltpu.VMEM((TPAD, 512), BF16),
            pltpu.VMEM((16, 8, 128), F32),
            dma,
            dma,
            pltpu.VMEM((2048, 1024), BF16),
            pltpu.VMEM((2048, 1024), BF16),
            pltpu.VMEM((224, 2, 128, 128), BF16),
            pltpu.VMEM((512, 2048), BF16),
            pltpu.VMEM((3, 32, 128), BF16),
            pltpu.VMEM((128, 128), F32),
            pltpu.VMEM((22, 32, 128), BF16),
            pltpu.VMEM((22, 32, 128), BF16),
            pltpu.VMEM((8, 8, 128), F32),
            pltpu.VMEM((8, 8, 128), BF16),
            pltpu.VMEM((8, 8, 128), BF16),
            pltpu.VMEM((64, 128), F32),
            pltpu.VMEM((4, 16, 128), BF16),
            pltpu.VMEM((16, 4, 16, 128), BF16),
            pltpu.VMEM((4, 256, 128), F32),
            pltpu.VMEM((8, 8, 128), F32),
            pltpu.VMEM((8, 8, 128), F32),
            pltpu.VMEM((32, 2048), BF16),
            pltpu.VMEM((1536, TPAD), BF16),
            pltpu.VMEM((1536, 1024), F32),
            pltpu.VMEM((704, 128), F32),
            pltpu.VMEM((4096, TPAD), BF16),
            pltpu.VMEM((4096, 512), F32),
            pltpu.VMEM((128, 128), F32),
            pltpu.VMEM((224, 256), F32),
            pltpu.VMEM((224, 512), BF16),
            dma((8,)),
            dma((8,)),
            dma((224 // GROUP,)),
            dma,
            dma,
            dma((2,)),
            dma((2,)),
            dma((22,)),
            dma((22,)),
            dma((8,)),
            dma((8,)),
            dma((16,)),
            dma((16,)),
            dma((8,)),
            dma((8,)),
        ],
        compiler_params=pltpu.CompilerParams(
            collective_id=0, has_side_effects=True, vmem_limit_bytes=58 * 1024 * 1024
        ),
    )(
        density.reshape(32, 128), send_box.reshape(128, 4).transpose(1, 0), near_src, near_tile,
        distant_pattern_slot, far_type, par_far, par_type, shift_rows,
        radiate.reshape(2048, 1024), receive.reshape(2048, 1024), near_tiles, interp_matrix, lo_rows, hi_rows,
    )
    return res.reshape(16, 2, 128)


def solution(mesh):
    both = ("box", "samp")
    return jax.shard_map(
        on_device,
        mesh=mesh,
        in_specs=(
            P(both, None, None), P(both, None, None), P(both, None, None), P(both, None, None, None),
            P(both, None), P(both, None), P(both, None, None), P(both, None), P(both, None),
            P(), P(), P(), P("box", None), P("box", None), P(),
        ),
        out_specs=P(both, None, None),
        check_vma=False,
    )
```

```python
import functools

import jax
import jax.numpy as jnp
from jax import lax
from jax.experimental import pallas as pl
from jax.experimental.pallas import tpu as pltpu
from jax.sharding import PartitionSpec as P

F32 = jnp.float32
BF16 = jnp.bfloat16
I32 = jnp.int32
JUMPS = (16, 32, 64, 96, 112)
TPAD = 384
GROUP = 16


def nn(a, b):
    return lax.dot_general(a, b, (((1,), (0,)), ((), ())), preferred_element_type=F32)


def nt(a, b):
    return lax.dot_general(a, b, (((1,), (1,)), ((), ())), preferred_element_type=F32)


def rows_of(shape):
    return lax.broadcasted_iota(I32, shape, 0)


def lanes_of(shape):
    return lax.broadcasted_iota(I32, shape, 1)


def onehot(mask):
    return jnp.where(mask, 1.0, 0.0).astype(BF16)


def device(pos):
    return (pos // 32, pos % 32)


def kernel(
    dens_h, sb, near_src_h, near_tile_h, dps_h, ftype_h, pfar_h, ptype_h, shift_h,
    radiate, receive, tiles, interp, lo_rows, hi_rows,
    out,
    dens, near_src, near_tile, dps_in, ftype_in, pfar_in, ptype_in, shift_rows, small_sem,
    dens_f, win_f, nidx, dps, ftype, pfar, ptype, shifts, lo_v, hi_v, hi_f, tlo, thi, pat3, lo_sem, hi_sem,
    rad_v, rec_v, tile_v, int_v, window, patf, leaf_msg, leaf_in, hi_scr, one_msg, one_in, one_f,
    two_msg, two_in, hi_p, ret_msg, ret_in, down, n_lo, w_lo, p_lo, n_hi, w_hi, inc_lo, contrib, picked,
    rad_sem, rec_sem, tile_sem, int_sem, loc_sem,
    win_s, win_r, leaf_s, leaf_r, one_s, one_r, two_s, two_r, ret_s, ret_r,
):
    y = lax.axis_index("box")
    s = lax.axis_index("samp")
    me = y * 32 + s
    zc = s % 8
    yx = y * 4 + s // 8

    def rad_copy(i):
        sl = pl.ds(i * 256, 256)
        return pltpu.make_async_copy(radiate.at[sl], rad_v.at[sl], rad_sem.at[i])

    def rec_copy(i):
        sl = pl.ds(i * 256, 256)
        return pltpu.make_async_copy(receive.at[sl], rec_v.at[sl], rec_sem.at[i])

    def tile_copy(i):
        sl = pl.ds(i * GROUP, GROUP)
        return pltpu.make_async_copy(tiles.at[sl], tile_v.at[sl], tile_sem.at[i])

    int_copy = pltpu.make_async_copy(interp, int_v, int_sem)
    groups = tiles.shape[0] // GROUP

    lo_copy = pltpu.make_async_copy(lo_rows, lo_v, lo_sem)
    hi_copy = pltpu.make_async_copy(hi_rows.at[:, pl.ds((zc // 4) * 16, 16), :], hi_v, hi_sem)

    column = s // 8
    part = pl.ds(pl.multiple_of(column * 16, 16), 16)
    small = [
        pltpu.make_async_copy(a, b, small_sem.at[i])
        for i, (a, b) in enumerate(
            (
                (dens_h, dens), (shift_h, shift_rows), (near_src_h, near_src), (near_tile_h, near_tile),
                (dps_h, dps_in), (ftype_h, ftype_in), (pfar_h.at[part], pfar_in), (ptype_h.at[part], ptype_in),
            )
        )
    ]
    small[0].start()
    for i in range(8):
        rad_copy(i).start()
    for c in small[1:]:
        c.start()
    int_copy.start()
    lo_copy.start()
    hi_copy.start()

    barrier = pltpu.get_barrier_semaphore()

    @pl.loop(1, 16)
    def _(i):
        pl.semaphore_signal(barrier, inc=1, device_id=device((me + 8 * i) % 128), device_id_type=pl.DeviceIdType.MESH)

    @pl.loop(1, 8)
    def _(i):
        pl.semaphore_signal(barrier, inc=1, device_id=device((me + i) % 128), device_id_type=pl.DeviceIdType.MESH)
        pl.semaphore_signal(barrier, inc=1, device_id=device((me + 128 - i) % 128), device_id_type=pl.DeviceIdType.MESH)

    small[0].wait()
    dens_f[...] = dens[...].astype(F32)
    d_re = dens_f[pl.ds(0, 16, stride=2), :]
    d_im = dens_f[pl.ds(1, 16, stride=2), :]
    d_all = jnp.concatenate([d_re, d_im], 0)
    own = rows_of((32, 128)) % 16
    acc = jnp.zeros((32, 1024), F32)
    for i in range(8):
        rad_copy(i).wait()
        lhs = jnp.concatenate(
            [jnp.where(own == 2 * i + h, d_all, 0.0).astype(BF16) for h in range(2)], 1
        )
        acc = acc + nn(lhs, rad_v[i * 256 : (i + 1) * 256])
    @pl.loop(0, groups)
    def _(i):
        tile_copy(i).start()

    @pl.loop(0, 8)
    def _(i):
        rec_copy(i).start()

    def send(src, dst, ss, rs, pos):
        return pltpu.make_async_remote_copy(
            src_ref=src, dst_ref=dst, send_sem=ss, recv_sem=rs, device_id=device(pos), device_id_type=pl.DeviceIdType.MESH
        )

    pat = jnp.concatenate([acc[:16, :512] - acc[16:, 512:], acc[:16, 512:] + acc[16:, :512]], 0).astype(BF16)
    pat_f = pat.astype(F32)
    for m in range(2):
        for b in range(4):
            patf[pl.ds(m * 4 + b, 16, stride=8), :] = pat_f[m * 16 : (m + 1) * 16, b * 128 : (b + 1) * 128]
    pat3[...] = patf[...].reshape(16, 8, 128)
    small[1].wait()
    for m in range(2):
        for b in range(16):
            shifts[m, :, b * 128 : (b + 1) * 128] = shift_rows[pl.ds(b * 2 + m, 8, stride=32), :]

    pl.semaphore_wait(barrier, 29)

    up_copy = send(dens, window.at[0], win_s.at[0], win_r.at[0], (me + 1) % 128)
    low_copy = send(dens, window.at[2], win_s.at[1], win_r.at[1], (me + 127) % 128)
    up_copy.start()
    low_copy.start()
    window[1] = dens[...]

    def fill(dst, j, receiver):
        for half in range(2):
            parts = []
            for k in range(2):
                box = jnp.minimum(sb[half * 2 + k, receiver], 15)
                parts.append(pat3[box])
            dst[j, pl.ds(half * 16, 16), :] = jnp.concatenate(parts, 0).astype(BF16)

    def near_send(j):
        return send(leaf_msg.at[j], leaf_in.at[16 - j], leaf_s.at[j], leaf_r.at[16 - j], (me + j + 120) % 128)

    def jump_send(i):
        return send(
            leaf_msg.at[17 + i], leaf_in.at[21 - i], leaf_s.at[17 + i], leaf_r.at[21 - i], (me + JUMPS[i]) % 128
        )

    int_copy.wait()
    up = nn(pat, int_v[...])
    s_re = shifts[0]
    s_im = shifts[1]
    for p in range(2):
        re = up[p * 8 : p * 8 + 8]
        im = up[16 + p * 8 : 24 + p * 8]
        vals = (
            jnp.sum(re * s_re - im * s_im, 0, keepdims=True),
            jnp.sum(re * s_im + im * s_re, 0, keepdims=True),
        )
        for m in range(2):
            for c in range(8):
                for h in range(2):
                    b = c * 2 + h
                    hi_scr[c, pl.ds(m * 4 + h * 2 + p, 1), :] = vals[m][:, b * 128 : (b + 1) * 128]
    one_msg[...] = hi_scr[...].astype(BF16)

    def one_send(i):
        peer = (zc + i) % 8
        return send(one_msg.at[peer], one_in.at[zc], one_s.at[i], one_r.at[i], yx * 8 + peer)

    @pl.loop(1, 8)
    def _(i):
        one_send(i).start()

    one_in[zc] = one_msg[zc]

    @pl.loop(0, 8)
    def _(j):
        fill(leaf_msg, j, (me + j + 120) % 128)
        near_send(j).start()

    @pl.loop(9, 17)
    def _(j):
        fill(leaf_msg, j, (me + j + 120) % 128)
        near_send(j).start()

    for i in range(5):
        fill(leaf_msg, 17 + i, (me + JUMPS[i]) % 128)
        jump_send(i).start()
    fill(leaf_in, 8, me)

    for c in small[2:]:
        c.wait()
    nidx[...] = jnp.full((8, 128), -1, I32)
    for g in range(16):
        at = (g % 4) * 32
        nidx[g // 4 : g // 4 + 1, at : at + 27] = near_src[g : g + 1, :]
        nidx[4 + g // 4 : 5 + g // 4, at : at + 27] = near_tile[g : g + 1, :]
    for held, given in ((dps, dps_in[...]), (ftype, ftype_in[...]), (pfar, pfar_in[...]), (ptype, ptype_in[...])):
        held[...] = jnp.full((16, 256), -1, I32)
        held[:, :189] = given
    hi_copy.wait()

    @pl.loop(0, 4)
    def _(i):
        hi_f[pl.ds(pl.multiple_of(i * 1264, 16), 1264), :] = hi_v[pl.ds(i * 79, 79)].astype(F32).reshape(1264, 128)

    hi_f[5056:, :] = jnp.zeros((1088, 128), F32)
    for r in range(4):
        at = (r % 2) * 256 + (r // 2) * 128
        thi[:, at : at + 128] = hi_f[pl.ds((zc % 4) * 4 + r, TPAD, stride=16), :].astype(BF16)

    kinds = rows_of((TPAD, 256))
    prow = rows_of((256, 256))
    parent = (prow // 16) * 16 + (prow % 8) * 2 + (prow // 8) % 2

    @pl.loop(0, 16, unroll=True)
    def _(g):
        a = onehot(pfar[pl.ds(g, 1), :] == parent)
        b = onehot(ptype[pl.ds(g, 1), :] == kinds)
        n_hi[pl.ds(pl.multiple_of(g * 256, 256), 256), :] = nt(a, b).astype(BF16)

    @pl.loop(1, 8)
    def _(i):
        one_send(i).wait_recv()

    one_f[...] = one_in[...].astype(F32).reshape(64, 128)
    for m in range(4):
        two_msg[m] = jnp.concatenate(
            [one_f[pl.ds(m * 2 + p, 8, stride=8), :] for p in range(2)], 0
        ).astype(BF16)

    def two_send(i):
        peer = (yx + i) % 16
        return send(two_msg, two_in.at[yx], two_s.at[i], two_r.at[i], peer * 8 + zc)

    @pl.loop(1, 16)
    def _(i):
        two_send(i).start()

    two_in[yx] = two_msg[...]

    w_hi[...] = nn(n_hi[...], thi[...])

    @pl.loop(1, 16)
    def _(i):
        two_send(i).wait_recv()

    for m in range(4):
        for i in range(16):
            hi_p[m, i * 16 : (i + 1) * 16, :] = two_in[i, m].astype(F32)

    @pl.loop(0, 8, unroll=2)
    def _(c):
        for p in range(2):
            base = pl.multiple_of((c * 2 + p) * 256, 256)
            for h in range(2):
                wr = w_hi[pl.ds(base, 256), h * 128 : (h + 1) * 128]
                wi = w_hi[pl.ds(base, 256), 256 + h * 128 : 256 + (h + 1) * 128]
                pr = hi_p[h]
                pi = hi_p[2 + h]
                ret_msg[c, pl.ds(h * 2 + p, 1), :] = jnp.sum(wr * pr - wi * pi, 0, keepdims=True)
                ret_msg[c, pl.ds(4 + h * 2 + p, 1), :] = jnp.sum(wr * pi + wi * pr, 0, keepdims=True)

    def ret_send(i):
        peer = (zc + i) % 8
        return send(ret_msg.at[peer], ret_in.at[zc], ret_s.at[i], ret_r.at[i], yx * 8 + peer)

    @pl.loop(1, 8)
    def _(i):
        ret_send(i).start()

    ret_in[zc] = ret_msg[zc]

    lo_copy.wait()
    hi_f[:2528, :] = lo_v[...].astype(F32)
    hi_f[2528:3072, :] = jnp.zeros((544, 128), F32)
    for r in range(8):
        at = (r % 2) * 512 + (r // 2) * 128
        tlo[:, at : at + 128] = hi_f[pl.ds(r, TPAD, stride=8), :].astype(BF16)

    row = rows_of((96, 256))
    slot = row // 4
    delta = jnp.where(
        slot <= 16,
        slot - 8,
        jnp.where(slot == 17, 16, jnp.where(slot == 18, 32, jnp.where(slot == 19, 64, jnp.where(slot == 20, 96, 112)))),
    )
    expect = jnp.where(row < 88, ((me + delta + 128) % 128) * 4 + row % 4, -2)

    @pl.loop(0, 16, unroll=True)
    def _(g):
        a = onehot(dps[pl.ds(g, 1), :] == expect)
        b = onehot(ftype[pl.ds(g, 1), :] == kinds)
        n_lo[pl.ds(pl.multiple_of(g * 96, 32), 96), :] = nt(a, b).astype(BF16)

    w_lo[...] = nn(n_lo[...], tlo[...])

    up_copy.wait_recv()
    low_copy.wait_recv()
    tile_rows = me * 224 + rows_of((224, 128))
    live = jnp.concatenate([onehot(nidx[pl.ds(4 + r, 1), :] == tile_rows) for r in range(4)], 1)
    box_rows = (me - 1) * 16 + rows_of((48, 128))
    source = jnp.concatenate([onehot(nidx[pl.ds(r, 1), :] == box_rows) for r in range(4)], 1)
    owner = jnp.concatenate(
        [onehot(rows_of((16, 128)) == 4 * r + lanes_of((16, 128)) // 32) for r in range(4)], 1
    )
    own_tile = nt(owner, live).astype(BF16)
    select = nt(live, source).astype(BF16)
    win_f[...] = window[...].astype(F32).reshape(96, 128)
    x_re = win_f[pl.ds(0, 48, stride=2), :]
    x_im = win_f[pl.ds(1, 48, stride=2), :]
    values = jnp.concatenate([x_re, -x_im, x_im, x_re], 1).astype(BF16)
    picked[...] = nn(select, values).astype(BF16)

    @pl.loop(0, groups)
    def _(grp):
        tile_copy(grp).wait()

    @pl.loop(0, groups, unroll=True)
    def _(grp):
        base = pl.multiple_of(grp * GROUP, GROUP)
        x = picked[pl.ds(base, GROUP), :]
        lhs = jnp.concatenate([x[:, :256], x[:, 256:]], 0)
        local = rows_of((2 * GROUP, 128)) % GROUP
        total = jnp.zeros((2 * GROUP, 128), F32)
        for q in range(GROUP // 2):
            pair = []
            for u in range(2):
                t = base + 2 * q + u
                pair.append(jnp.concatenate([tile_v[t, 0], tile_v[t, 1]], 1))
            res = nt(lhs, jnp.concatenate(pair, 0))
            for u in range(2):
                total = total + jnp.where(local == 2 * q + u, res[:, u * 128 : (u + 1) * 128], 0.0)
        contrib[pl.ds(base, GROUP), :] = jnp.concatenate([total[:GROUP], total[GROUP:]], 1)

    whole = contrib[...]
    high = whole.astype(BF16)
    near = nn(own_tile, high) + nn(own_tile, (whole - high.astype(F32)).astype(BF16))

    @pl.loop(0, 8)
    def _(j):
        near_send(j).wait_recv()

    @pl.loop(9, 17)
    def _(j):
        near_send(j).wait_recv()

    for i in range(5):
        jump_send(i).wait_recv()

    p_lo[...] = leaf_in[...].astype(F32).reshape(704, 128)

    @pl.loop(0, 16, unroll=2)
    def _(g):
        base = pl.multiple_of(g * 96, 32)
        reals, imags = [], []
        for b in range(4):
            wr = w_lo[pl.ds(base, 88), b * 128 : (b + 1) * 128]
            wi = w_lo[pl.ds(base, 88), 512 + b * 128 : 512 + (b + 1) * 128]
            pr = p_lo[pl.ds(b, 88, stride=8), :]
            pi = p_lo[pl.ds(4 + b, 88, stride=8), :]
            reals.append(jnp.sum(wr * pr - wi * pi, 0, keepdims=True))
            imags.append(jnp.sum(wr * pi + wi * pr, 0, keepdims=True))
        inc_lo[pl.ds(pl.multiple_of(g * 8, 8), 8), :] = jnp.concatenate(reals + imags, 0)

    @pl.loop(1, 8)
    def _(i):
        ret_send(i).wait_recv()

    for c in range(8):
        for h in range(2):
            b = c * 2 + h
            sr = shifts[0, :, b * 128 : (b + 1) * 128]
            si = shifts[1, :, b * 128 : (b + 1) * 128]
            parts = ([], [])
            for p in range(2):
                ir = ret_in[c, pl.ds(h * 2 + p, 1), :]
                ii = ret_in[c, pl.ds(4 + h * 2 + p, 1), :]
                parts[0].append(sr * ir + si * ii)
                parts[1].append(sr * ii - si * ir)
            for m in range(2):
                down[m * 16 : (m + 1) * 16, b * 128 : (b + 1) * 128] = jnp.concatenate(parts[m], 0).astype(BF16)
    direct = jnp.concatenate(
        [
            jnp.concatenate([inc_lo[pl.ds(m * 4 + b, 16, stride=8), :] for b in range(4)], 1)
            for m in range(2)
        ],
        0,
    )
    incoming = (direct + nt(down[...], int_v[...])).astype(BF16)
    in_re = incoming[:16]
    in_im = incoming[16:]
    lhs = jnp.concatenate([jnp.concatenate([in_re, -in_im], 1), jnp.concatenate([in_im, in_re], 1)], 0)
    far = jnp.zeros((32, 128), F32)
    for i in range(8):
        rec_copy(i).wait()
        res = nt(lhs, rec_v[i * 256 : (i + 1) * 256])
        for u in range(2):
            far = far + jnp.where(own == 2 * i + u, res[:, u * 128 : (u + 1) * 128], 0.0)
    out[pl.ds(0, 16, stride=2), :] = near[:, :128] + far[:16]
    out[pl.ds(1, 16, stride=2), :] = near[:, 128:] + far[16:]

    up_copy.wait_send()
    low_copy.wait_send()

    @pl.loop(1, 8)
    def _(i):
        one_send(i).wait_send()
        ret_send(i).wait_send()

    @pl.loop(1, 16)
    def _(i):
        two_send(i).wait_send()

    @pl.loop(0, 8)
    def _(j):
        near_send(j).wait_send()

    @pl.loop(9, 17)
    def _(j):
        near_send(j).wait_send()

    for i in range(5):
        jump_send(i).wait_send()


def on_device(
    density, radiate, receive, near_tiles, near_src, near_tile, send_box, distant_pattern_slot, far_type,
    trans_lo, interp_matrix, shifts, par_far, par_type, trans_hi,
):
    types = trans_lo.shape[0]
    lo_rows = trans_lo.reshape(types, 2, 4, 128).transpose(0, 2, 1, 3).reshape(types * 8, 128)
    hi_rows = trans_hi.reshape(types, 2, 16, 128).transpose(0, 2, 1, 3).reshape(types, 32, 128)
    shift_rows = shifts.reshape(8, 2, 16, 128).transpose(0, 2, 1, 3).reshape(256, 128)

    vm = pl.BlockSpec(memory_space=pltpu.VMEM)
    anyspace = pl.BlockSpec(memory_space=pl.ANY)
    dma = pltpu.SemaphoreType.DMA
    res = pl.pallas_call(
        kernel,
        name="mlfmm",
        out_shape=jax.ShapeDtypeStruct((32, 128), F32),
        in_specs=[anyspace, pl.BlockSpec(memory_space=pltpu.SMEM)] + [anyspace] * 13,
        out_specs=vm,
        scratch_shapes=[
            pltpu.VMEM((32, 128), BF16),
            pltpu.VMEM((16, 27), I32),
            pltpu.VMEM((16, 27), I32),
            pltpu.VMEM((16, 189), I32),
            pltpu.VMEM((16, 189), I32),
            pltpu.VMEM((16, 189), I32),
            pltpu.VMEM((16, 189), I32),
            pltpu.VMEM((256, 128), F32),
            dma((8,)),
            pltpu.VMEM((32, 128), F32),
            pltpu.VMEM((96, 128), F32),
            pltpu.VMEM((8, 128), I32),
            pltpu.VMEM((16, 256), I32),
            pltpu.VMEM((16, 256), I32),
            pltpu.VMEM((16, 256), I32),
            pltpu.VMEM((16, 256), I32),
            pltpu.VMEM((2, 8, 2048), F32),
            pltpu.VMEM((2528, 128), BF16),
            pltpu.VMEM((316, 16, 128), BF16),
            pltpu.VMEM((TPAD * 16, 128), F32),
            pltpu.VMEM((TPAD, 1024), BF16),
            pltpu.VMEM((TPAD, 512), BF16),
            pltpu.VMEM((16, 8, 128), F32),
            dma,
            dma,
            pltpu.VMEM((2048, 1024), BF16),
            pltpu.VMEM((2048, 1024), BF16),
            pltpu.VMEM((224, 2, 128, 128), BF16),
            pltpu.VMEM((512, 2048), BF16),
            pltpu.VMEM((3, 32, 128), BF16),
            pltpu.VMEM((128, 128), F32),
            pltpu.VMEM((22, 32, 128), BF16),
            pltpu.VMEM((22, 32, 128), BF16),
            pltpu.VMEM((8, 8, 128), F32),
            pltpu.VMEM((8, 8, 128), BF16),
            pltpu.VMEM((8, 8, 128), BF16),
            pltpu.VMEM((64, 128), F32),
            pltpu.VMEM((4, 16, 128), BF16),
            pltpu.VMEM((16, 4, 16, 128), BF16),
            pltpu.VMEM((4, 256, 128), F32),
            pltpu.VMEM((8, 8, 128), F32),
            pltpu.VMEM((8, 8, 128), F32),
            pltpu.VMEM((32, 2048), BF16),
            pltpu.VMEM((1536, TPAD), BF16),
            pltpu.VMEM((1536, 1024), F32),
            pltpu.VMEM((704, 128), F32),
            pltpu.VMEM((4096, TPAD), BF16),
            pltpu.VMEM((4096, 512), F32),
            pltpu.VMEM((128, 128), F32),
            pltpu.VMEM((224, 256), F32),
            pltpu.VMEM((224, 512), BF16),
            dma((8,)),
            dma((8,)),
            dma((224 // GROUP,)),
            dma,
            dma,
            dma((2,)),
            dma((2,)),
            dma((22,)),
            dma((22,)),
            dma((8,)),
            dma((8,)),
            dma((16,)),
            dma((16,)),
            dma((8,)),
            dma((8,)),
        ],
        compiler_params=pltpu.CompilerParams(
            collective_id=0, has_side_effects=True, vmem_limit_bytes=59 * 1024 * 1024
        ),
    )(
        density.reshape(32, 128), send_box.reshape(128, 4).transpose(1, 0), near_src, near_tile,
        distant_pattern_slot, far_type, par_far, par_type, shift_rows,
        radiate.reshape(2048, 1024), receive.reshape(2048, 1024), near_tiles, interp_matrix, lo_rows, hi_rows,
    )
    return (res + 0.5 * density.reshape(32, 128).astype(F32)).reshape(16, 2, 128)


def solution(mesh):
    both = ("box", "samp")
    return jax.shard_map(
        on_device,
        mesh=mesh,
        in_specs=(
            P(both, None, None), P(both, None, None), P(both, None, None), P(both, None, None, None),
            P(both, None), P(both, None), P(both, None, None), P(both, None), P(both, None),
            P(), P(), P(), P("box", None), P("box", None), P(),
        ),
        out_specs=P(both, None, None),
        check_vma=False,
    )
```

```python
import functools

import jax
import jax.numpy as jnp
from jax import lax
from jax.experimental import pallas as pl
from jax.experimental.pallas import tpu as pltpu
from jax.sharding import PartitionSpec as P

F32 = jnp.float32
BF16 = jnp.bfloat16
I32 = jnp.int32
JUMPS = (16, 32, 64, 96, 112)
TPAD = 384
GROUP = 16


def nn(a, b):
    return lax.dot_general(a, b, (((1,), (0,)), ((), ())), preferred_element_type=F32)


def nt(a, b):
    return lax.dot_general(a, b, (((1,), (1,)), ((), ())), preferred_element_type=F32)


def rows_of(shape):
    return lax.broadcasted_iota(I32, shape, 0)


def lanes_of(shape):
    return lax.broadcasted_iota(I32, shape, 1)


def onehot(mask):
    return jnp.where(mask, 1.0, 0.0).astype(BF16)


def device(pos):
    return (pos // 32, pos % 32)


def kernel(
    dens_h, sb, near_src_h, near_tile_h, dps_h, ftype_h, pfar_h, ptype_h, shift_h,
    radiate, receive, tiles, interp, lo_rows, hi_rows,
    out,
    dens, near_src, near_tile, dps_in, ftype_in, pfar_in, ptype_in, shift_rows, small_sem,
    dens_f, win_f, nidx, dps, ftype, pfar, ptype, shifts, lo_v, hi_v, hi_f, tlo, thi, pat3, lo_sem, hi_sem,
    rad_v, rec_v, tile_v, int_v, window, patf, leaf_msg, leaf_in, hi_scr, one_msg, one_in, one_f,
    two_msg, two_in, hi_p, ret_msg, ret_in, down, n_lo, w_lo, p_lo, n_hi, w_hi, inc_lo, contrib, picked,
    rad_sem, rec_sem, tile_sem, int_sem, loc_sem,
    win_s, win_r, leaf_s, leaf_r, one_s, one_r, two_s, two_r, ret_s, ret_r,
):
    y = lax.axis_index("box")
    s = lax.axis_index("samp")
    me = y * 32 + s
    zc = s % 8
    yx = y * 4 + s // 8

    rad_copy = pltpu.make_async_copy(radiate, rad_v, rad_sem)
    rec_copy = pltpu.make_async_copy(receive, rec_v, rec_sem)
    tile_copy = pltpu.make_async_copy(tiles, tile_v, tile_sem)
    int_copy = pltpu.make_async_copy(interp, int_v, int_sem)
    groups = tiles.shape[0] // GROUP

    lo_copy = pltpu.make_async_copy(lo_rows, lo_v, lo_sem)
    hi_copy = pltpu.make_async_copy(hi_rows.at[:, pl.ds((zc // 4) * 16, 16), :], hi_v, hi_sem)

    column = s // 8
    part = pl.ds(pl.multiple_of(column * 16, 16), 16)
    small = [
        pltpu.make_async_copy(a, b, small_sem.at[i])
        for i, (a, b) in enumerate(
            (
                (dens_h, dens), (shift_h, shift_rows), (near_src_h, near_src), (near_tile_h, near_tile),
                (dps_h, dps_in), (ftype_h, ftype_in), (pfar_h.at[part], pfar_in), (ptype_h.at[part], ptype_in),
            )
        )
    ]
    for c in small:
        c.start()
    rad_copy.start()
    int_copy.start()
    lo_copy.start()
    hi_copy.start()

    barrier = pltpu.get_barrier_semaphore()

    @pl.loop(1, 16, unroll=True)
    def _(i):
        pl.semaphore_signal(barrier, inc=1, device_id=device((me + 8 * i) % 128), device_id_type=pl.DeviceIdType.MESH)

    @pl.loop(1, 8, unroll=True)
    def _(i):
        pl.semaphore_signal(barrier, inc=1, device_id=device((me + i) % 128), device_id_type=pl.DeviceIdType.MESH)
        pl.semaphore_signal(barrier, inc=1, device_id=device((me + 128 - i) % 128), device_id_type=pl.DeviceIdType.MESH)

    for c in small[2:]:
        c.wait()
    nidx[...] = jnp.full((8, 128), -1, I32)
    for g in range(16):
        at = (g % 4) * 32
        nidx[g // 4 : g // 4 + 1, at : at + 27] = near_src[g : g + 1, :]
        nidx[4 + g // 4 : 5 + g // 4, at : at + 27] = near_tile[g : g + 1, :]
    for held, given in ((dps, dps_in[...]), (ftype, ftype_in[...]), (pfar, pfar_in[...]), (ptype, ptype_in[...])):
        held[...] = jnp.full((16, 256), -1, I32)
        held[:, :189] = given

    kinds = rows_of((TPAD, 256))
    prow = rows_of((256, 256))
    parent = (prow // 16) * 16 + (prow % 8) * 2 + (prow // 8) % 2

    @pl.loop(0, 16, unroll=True)
    def _(g):
        a = onehot(pfar[pl.ds(g, 1), :] == parent)
        b = onehot(ptype[pl.ds(g, 1), :] == kinds)
        n_hi[pl.ds(pl.multiple_of(g * 256, 256), 256), :] = nt(a, b).astype(BF16)

    small[0].wait()
    dens_f[...] = dens[...].astype(F32)
    d_re = dens_f[pl.ds(0, 16, stride=2), :]
    d_im = dens_f[pl.ds(1, 16, stride=2), :]
    d_all = jnp.concatenate([d_re, d_im], 0)
    own = rows_of((32, 128)) % 16
    acc = jnp.zeros((32, 1024), F32)
    rad_copy.wait()
    for i in range(8):
        lhs = jnp.concatenate(
            [jnp.where(own == 2 * i + h, d_all, 0.0).astype(BF16) for h in range(2)], 1
        )
        acc = acc + nn(lhs, rad_v[i * 256 : (i + 1) * 256])
    tile_copy.start()
    rec_copy.start()
    def send(src, dst, ss, rs, pos):
        return pltpu.make_async_remote_copy(
            src_ref=src, dst_ref=dst, send_sem=ss, recv_sem=rs, device_id=device(pos), device_id_type=pl.DeviceIdType.MESH
        )

    pat = jnp.concatenate([acc[:16, :512] - acc[16:, 512:], acc[:16, 512:] + acc[16:, :512]], 0).astype(BF16)
    pat_f = pat.astype(F32)
    for m in range(2):
        for b in range(4):
            patf[pl.ds(m * 4 + b, 16, stride=8), :] = pat_f[m * 16 : (m + 1) * 16, b * 128 : (b + 1) * 128]
    pat3[...] = patf[...].reshape(16, 8, 128)
    small[1].wait()
    for m in range(2):
        for b in range(16):
            shifts[m, :, b * 128 : (b + 1) * 128] = shift_rows[pl.ds(b * 2 + m, 8, stride=32), :]

    pl.semaphore_wait(barrier, 29)

    up_copy = send(dens, window.at[0], win_s, win_r, (me + 1) % 128)
    low_copy = send(dens, window.at[2], win_s, win_r, (me + 127) % 128)
    up_copy.start()
    low_copy.start()
    window[1] = dens[...]

    def wait_for(ref, copies, sem):
        part = ref.at[pl.ds(0, copies)]
        pltpu.make_async_copy(part, part, sem).wait()

    def fill(dst, j, receiver):
        for half in range(2):
            parts = []
            for k in range(2):
                box = jnp.minimum(sb[half * 2 + k, receiver], 15)
                parts.append(pat3[box])
            dst[j, pl.ds(half * 16, 16), :] = jnp.concatenate(parts, 0).astype(BF16)

    def near_send(j):
        return send(leaf_msg.at[j], leaf_in.at[16 - j], leaf_s, leaf_r, (me + j + 120) % 128)

    def jump_send(i):
        return send(
            leaf_msg.at[17 + i], leaf_in.at[21 - i], leaf_s, leaf_r, (me + JUMPS[i]) % 128
        )

    int_copy.wait()
    up = nn(pat, int_v[...])
    s_re = shifts[0]
    s_im = shifts[1]
    for p in range(2):
        re = up[p * 8 : p * 8 + 8]
        im = up[16 + p * 8 : 24 + p * 8]
        vals = (
            jnp.sum(re * s_re - im * s_im, 0, keepdims=True),
            jnp.sum(re * s_im + im * s_re, 0, keepdims=True),
        )
        for m in range(2):
            for c in range(8):
                for h in range(2):
                    b = c * 2 + h
                    hi_scr[c, pl.ds(m * 4 + h * 2 + p, 1), :] = vals[m][:, b * 128 : (b + 1) * 128]
    one_msg[...] = hi_scr[...].astype(BF16)

    def one_send(i):
        peer = (zc + i) % 8
        return send(one_msg.at[peer], one_in.at[zc], one_s, one_r, yx * 8 + peer)

    @pl.loop(1, 8)
    def _(i):
        one_send(i).start()

    one_in[zc] = one_msg[zc]

    @pl.loop(0, 8)
    def _(j):
        fill(leaf_msg, j, (me + j + 120) % 128)
        near_send(j).start()

    @pl.loop(9, 17)
    def _(j):
        fill(leaf_msg, j, (me + j + 120) % 128)
        near_send(j).start()

    for i in range(5):
        fill(leaf_msg, 17 + i, (me + JUMPS[i]) % 128)
        jump_send(i).start()
    fill(leaf_in, 8, me)

    hi_copy.wait()

    @pl.loop(0, 4)
    def _(i):
        hi_f[pl.ds(pl.multiple_of(i * 1264, 16), 1264), :] = hi_v[pl.ds(i * 79, 79)].astype(F32).reshape(1264, 128)

    hi_f[5056:, :] = jnp.zeros((1088, 128), F32)
    for r in range(4):
        at = (r % 2) * 256 + (r // 2) * 128
        thi[:, at : at + 128] = hi_f[pl.ds((zc % 4) * 4 + r, TPAD, stride=16), :].astype(BF16)

    lo_copy.wait()
    hi_f[:2528, :] = lo_v[...].astype(F32)
    hi_f[2528:3072, :] = jnp.zeros((544, 128), F32)
    for r in range(8):
        at = (r % 2) * 512 + (r // 2) * 128
        tlo[:, at : at + 128] = hi_f[pl.ds(r, TPAD, stride=8), :].astype(BF16)

    wait_for(one_in, 7, one_r)

    one_f[...] = one_in[...].astype(F32).reshape(64, 128)
    for m in range(4):
        two_msg[m] = jnp.concatenate(
            [one_f[pl.ds(m * 2 + p, 8, stride=8), :] for p in range(2)], 0
        ).astype(BF16)

    def two_send(i):
        peer = (yx + i) % 16
        return send(two_msg, two_in.at[yx], two_s, two_r, peer * 8 + zc)

    @pl.loop(1, 16)
    def _(i):
        two_send(i).start()

    two_in[yx] = two_msg[...]

    w_hi[...] = nn(n_hi[...], thi[...])

    row = rows_of((96, 256))
    slot = row // 4
    delta = jnp.where(
        slot <= 16,
        slot - 8,
        jnp.where(slot == 17, 16, jnp.where(slot == 18, 32, jnp.where(slot == 19, 64, jnp.where(slot == 20, 96, 112)))),
    )
    expect = jnp.where(row < 88, ((me + delta + 128) % 128) * 4 + row % 4, -2)

    @pl.loop(0, 16, unroll=True)
    def _(g):
        a = onehot(dps[pl.ds(g, 1), :] == expect)
        b = onehot(ftype[pl.ds(g, 1), :] == kinds)
        n_lo[pl.ds(pl.multiple_of(g * 96, 32), 96), :] = nt(a, b).astype(BF16)

    w_lo[...] = nn(n_lo[...], tlo[...])

    wait_for(two_in, 15, two_r)

    for m in range(4):
        for i in range(16):
            hi_p[m, i * 16 : (i + 1) * 16, :] = two_in[i, m].astype(F32)

    for c in range(8):
        for p in range(2):
            base = (c * 2 + p) * 256
            for h in range(2):
                wr = w_hi[base : base + 256, h * 128 : (h + 1) * 128]
                wi = w_hi[base : base + 256, 256 + h * 128 : 256 + (h + 1) * 128]
                pr = hi_p[h]
                pi = hi_p[2 + h]
                ret_msg[c, pl.ds(h * 2 + p, 1), :] = jnp.sum(wr * pr - wi * pi, 0, keepdims=True)
                ret_msg[c, pl.ds(4 + h * 2 + p, 1), :] = jnp.sum(wr * pi + wi * pr, 0, keepdims=True)

    def ret_send(i):
        peer = (zc + i) % 8
        return send(ret_msg.at[peer], ret_in.at[zc], ret_s, ret_r, yx * 8 + peer)

    @pl.loop(1, 8)
    def _(i):
        ret_send(i).start()

    ret_in[zc] = ret_msg[zc]

    wait_for(leaf_in, 21, leaf_r)
    p_lo[...] = leaf_in[...].astype(F32).reshape(704, 128)

    wait_for(window, 2, win_r)
    tile_rows = me * 224 + rows_of((224, 128))
    live = jnp.concatenate([onehot(nidx[pl.ds(4 + r, 1), :] == tile_rows) for r in range(4)], 1)
    box_rows = (me - 1) * 16 + rows_of((48, 128))
    source = jnp.concatenate([onehot(nidx[pl.ds(r, 1), :] == box_rows) for r in range(4)], 1)
    owner = jnp.concatenate(
        [onehot(rows_of((16, 128)) == 4 * r + lanes_of((16, 128)) // 32) for r in range(4)], 1
    )
    own_tile = nt(owner, live).astype(BF16)
    select = nt(live, source).astype(BF16)
    win_f[...] = window[...].astype(F32).reshape(96, 128)
    x_re = win_f[pl.ds(0, 48, stride=2), :]
    x_im = win_f[pl.ds(1, 48, stride=2), :]
    values = jnp.concatenate([x_re, -x_im, x_im, x_re], 1).astype(BF16)
    picked[...] = nn(select, values).astype(BF16)

    tile_copy.wait()
    def leaf_sum(g):
        base = g * 96
        reals, imags = [], []
        for b in range(4):
            wr = w_lo[base : base + 88, b * 128 : (b + 1) * 128]
            wi = w_lo[base : base + 88, 512 + b * 128 : 512 + (b + 1) * 128]
            pr = p_lo[pl.ds(b, 88, stride=8), :]
            pi = p_lo[pl.ds(4 + b, 88, stride=8), :]
            reals.append(jnp.sum(wr * pr - wi * pi, 0, keepdims=True))
            imags.append(jnp.sum(wr * pi + wi * pr, 0, keepdims=True))
        inc_lo[g * 8 : g * 8 + 8, :] = jnp.concatenate(reals + imags, 0)

    for grp in range(groups):
        base = grp * GROUP
        x = picked[base : base + GROUP, :]
        lhs = jnp.concatenate([x[:, :256], x[:, 256:]], 0)
        local = rows_of((2 * GROUP, 128)) % GROUP
        total = jnp.zeros((2 * GROUP, 128), F32)
        for q in range(GROUP // 2):
            pair = []
            for u in range(2):
                t = base + 2 * q + u
                pair.append(jnp.concatenate([tile_v[t, 0], tile_v[t, 1]], 1))
            res = nt(lhs, jnp.concatenate(pair, 0))
            for u in range(2):
                total = total + jnp.where(local == 2 * q + u, res[:, u * 128 : (u + 1) * 128], 0.0)
        contrib[base : base + GROUP, :] = jnp.concatenate([total[:GROUP], total[GROUP:]], 1)
        leaf_sum(grp)

    for g in range(groups, 16):
        leaf_sum(g)

    whole = contrib[...]
    high = whole.astype(BF16)
    near = nn(own_tile, high) + nn(own_tile, (whole - high.astype(F32)).astype(BF16))

    wait_for(window, 2, win_s)
    wait_for(one_in, 7, one_s)
    wait_for(two_in, 15, two_s)
    wait_for(leaf_in, 21, leaf_s)
    wait_for(ret_in, 7, ret_s)

    wait_for(ret_in, 7, ret_r)

    for c in range(8):
        for h in range(2):
            b = c * 2 + h
            sr = shifts[0, :, b * 128 : (b + 1) * 128]
            si = shifts[1, :, b * 128 : (b + 1) * 128]
            parts = ([], [])
            for p in range(2):
                ir = ret_in[c, pl.ds(h * 2 + p, 1), :]
                ii = ret_in[c, pl.ds(4 + h * 2 + p, 1), :]
                parts[0].append(sr * ir + si * ii)
                parts[1].append(sr * ii - si * ir)
            for m in range(2):
                down[m * 16 : (m + 1) * 16, b * 128 : (b + 1) * 128] = jnp.concatenate(parts[m], 0).astype(BF16)
    direct = jnp.concatenate(
        [
            jnp.concatenate([inc_lo[pl.ds(m * 4 + b, 16, stride=8), :] for b in range(4)], 1)
            for m in range(2)
        ],
        0,
    )
    incoming = (direct + nt(down[...], int_v[...])).astype(BF16)
    in_re = incoming[:16]
    in_im = incoming[16:]
    lhs = jnp.concatenate([jnp.concatenate([in_re, -in_im], 1), jnp.concatenate([in_im, in_re], 1)], 0)
    far = jnp.zeros((32, 128), F32)
    rec_copy.wait()
    for i in range(8):
        res = nt(lhs, rec_v[i * 256 : (i + 1) * 256])
        for u in range(2):
            far = far + jnp.where(own == 2 * i + u, res[:, u * 128 : (u + 1) * 128], 0.0)
    out[pl.ds(0, 16, stride=2), :] = near[:, :128] + far[:16]
    out[pl.ds(1, 16, stride=2), :] = near[:, 128:] + far[16:]


def on_device(
    density, radiate, receive, near_tiles, near_src, near_tile, send_box, distant_pattern_slot, far_type,
    trans_lo, interp_matrix, shifts, par_far, par_type, trans_hi,
):
    types = trans_lo.shape[0]
    lo_rows = trans_lo.reshape(types, 2, 4, 128).transpose(0, 2, 1, 3).reshape(types * 8, 128)
    hi_rows = trans_hi.reshape(types, 2, 16, 128).transpose(0, 2, 1, 3).reshape(types, 32, 128)
    shift_rows = shifts.reshape(8, 2, 16, 128).transpose(0, 2, 1, 3).reshape(256, 128)

    vm = pl.BlockSpec(memory_space=pltpu.VMEM)
    anyspace = pl.BlockSpec(memory_space=pl.ANY)
    dma = pltpu.SemaphoreType.DMA
    res = pl.pallas_call(
        kernel,
        name="mlfmm",
        out_shape=pltpu.VMEM((32, 128), F32),
        in_specs=[anyspace, pl.BlockSpec(memory_space=pltpu.SMEM)] + [anyspace] * 13,
        out_specs=vm,
        scratch_shapes=[
            pltpu.VMEM((32, 128), BF16),
            pltpu.VMEM((16, 27), I32),
            pltpu.VMEM((16, 27), I32),
            pltpu.VMEM((16, 189), I32),
            pltpu.VMEM((16, 189), I32),
            pltpu.VMEM((16, 189), I32),
            pltpu.VMEM((16, 189), I32),
            pltpu.VMEM((256, 128), F32),
            dma((8,)),
            pltpu.VMEM((32, 128), F32),
            pltpu.VMEM((96, 128), F32),
            pltpu.VMEM((8, 128), I32),
            pltpu.VMEM((16, 256), I32),
            pltpu.VMEM((16, 256), I32),
            pltpu.VMEM((16, 256), I32),
            pltpu.VMEM((16, 256), I32),
            pltpu.VMEM((2, 8, 2048), F32),
            pltpu.VMEM((2528, 128), BF16),
            pltpu.VMEM((316, 16, 128), BF16),
            pltpu.VMEM((TPAD * 16, 128), F32),
            pltpu.VMEM((TPAD, 1024), BF16),
            pltpu.VMEM((TPAD, 512), BF16),
            pltpu.VMEM((16, 8, 128), F32),
            dma,
            dma,
            pltpu.VMEM((2048, 1024), BF16),
            pltpu.VMEM((2048, 1024), BF16),
            pltpu.VMEM((224, 2, 128, 128), BF16),
            pltpu.VMEM((512, 2048), BF16),
            pltpu.VMEM((3, 32, 128), BF16),
            pltpu.VMEM((128, 128), F32),
            pltpu.VMEM((22, 32, 128), BF16),
            pltpu.VMEM((22, 32, 128), BF16),
            pltpu.VMEM((8, 8, 128), F32),
            pltpu.VMEM((8, 8, 128), BF16),
            pltpu.VMEM((8, 8, 128), BF16),
            pltpu.VMEM((64, 128), F32),
            pltpu.VMEM((4, 16, 128), BF16),
            pltpu.VMEM((16, 4, 16, 128), BF16),
            pltpu.VMEM((4, 256, 128), F32),
            pltpu.VMEM((8, 8, 128), F32),
            pltpu.VMEM((8, 8, 128), F32),
            pltpu.VMEM((32, 2048), BF16),
            pltpu.VMEM((1536, TPAD), BF16),
            pltpu.VMEM((1536, 1024), F32),
            pltpu.VMEM((704, 128), F32),
            pltpu.VMEM((4096, TPAD), BF16),
            pltpu.VMEM((4096, 512), F32),
            pltpu.VMEM((128, 128), F32),
            pltpu.VMEM((224, 256), F32),
            pltpu.VMEM((224, 512), BF16),
            dma,
            dma,
            dma,
            dma,
            dma,
            dma,
            dma,
            dma,
            dma,
            dma,
            dma,
            dma,
            dma,
            dma,
            dma,
        ],
        compiler_params=pltpu.CompilerParams(
            collective_id=0, has_side_effects=True, vmem_limit_bytes=59 * 1024 * 1024
        ),
    )(
        density.reshape(32, 128), send_box.reshape(128, 4).transpose(1, 0), near_src, near_tile,
        distant_pattern_slot, far_type, par_far, par_type, shift_rows,
        radiate.reshape(2048, 1024), receive.reshape(2048, 1024), near_tiles, interp_matrix, lo_rows, hi_rows,
    )
    return (res + 0.5 * density.reshape(32, 128).astype(F32)).reshape(16, 2, 128)


def solution(mesh):
    both = ("box", "samp")
    return jax.shard_map(
        on_device,
        mesh=mesh,
        in_specs=(
            P(both, None, None), P(both, None, None), P(both, None, None), P(both, None, None, None),
            P(both, None), P(both, None), P(both, None, None), P(both, None), P(both, None),
            P(), P(), P(), P("box", None), P("box", None), P(),
        ),
        out_specs=P(both, None, None),
        check_vma=False,
    )
```

```python
import functools

import jax
import jax.numpy as jnp
from jax import lax
from jax.experimental import pallas as pl
from jax.experimental.pallas import tpu as pltpu
from jax.sharding import PartitionSpec as P

F32 = jnp.float32
BF16 = jnp.bfloat16
I32 = jnp.int32
JUMPS = (16, 32, 64, 96, 112)
TPAD = 384
GROUP = 16


def nn(a, b):
    return lax.dot_general(a, b, (((1,), (0,)), ((), ())), preferred_element_type=F32)


def nt(a, b):
    return lax.dot_general(a, b, (((1,), (1,)), ((), ())), preferred_element_type=F32)


def rows_of(shape):
    return lax.broadcasted_iota(I32, shape, 0)


def lanes_of(shape):
    return lax.broadcasted_iota(I32, shape, 1)


def onehot(mask):
    return jnp.where(mask, 1.0, 0.0).astype(BF16)


def device(pos):
    return (pos // 32, pos % 32)


def kernel(
    dens_h, sb, near_src_h, near_tile_h, dps_h, ftype_h, pfar_h, ptype_h, shift_h,
    radiate, receive, tiles, interp, lo_rows, hi_rows,
    out,
    dens, near_src, near_tile, dps_in, ftype_in, pfar_in, ptype_in, shift_rows, small_sem,
    dens_f, win_f, nidx, dps, ftype, pfar, ptype, shifts, lo_v, hi_v, hi_f, tlo, thi, pat3, lo_sem, hi_sem,
    rad_v, rec_v, tile_v, int_v, window, patf, leaf_msg, leaf_in, hi_scr, one_msg, one_in, one_f,
    two_msg, two_in, hi_p, ret_msg, ret_in, down, n_lo, w_lo, p_lo, n_hi, w_hi, inc_lo, contrib, picked,
    rad_sem, rec_sem, tile_sem, int_sem, loc_sem,
    win_s, win_r, leaf_s, leaf_r, one_s, one_r, two_s, two_r, ret_s, ret_r,
):
    y = lax.axis_index("box")
    s = lax.axis_index("samp")
    me = y * 32 + s
    zc = s % 8
    yx = y * 4 + s // 8

    rad_copy = pltpu.make_async_copy(radiate, rad_v, rad_sem)
    rec_copy = pltpu.make_async_copy(receive, rec_v, rec_sem)
    tile_copy = pltpu.make_async_copy(tiles, tile_v, tile_sem)
    int_copy = pltpu.make_async_copy(interp, int_v, int_sem)
    groups = tiles.shape[0] // GROUP

    lo_copy = pltpu.make_async_copy(lo_rows, lo_v, lo_sem)
    hi_copy = pltpu.make_async_copy(hi_rows.at[:, pl.ds((zc // 4) * 16, 16), :], hi_v, hi_sem)

    column = s // 8
    part = pl.ds(pl.multiple_of(column * 16, 16), 16)
    small = [
        pltpu.make_async_copy(a, b, small_sem.at[i])
        for i, (a, b) in enumerate(
            (
                (pfar_h.at[part], pfar_in), (ptype_h.at[part], ptype_in), (dens_h, dens), (shift_h, shift_rows),
                (near_src_h, near_src), (near_tile_h, near_tile), (dps_h, dps_in), (ftype_h, ftype_in),
            )
        )
    ]
    for c in small[:3]:
        c.start()
    rad_copy.start()
    int_copy.start()
    for c in small[3:]:
        c.start()
    lo_copy.start()
    hi_copy.start()

    barrier = pltpu.get_barrier_semaphore()

    @pl.loop(1, 16, unroll=True)
    def _(i):
        pl.semaphore_signal(barrier, inc=1, device_id=device((me + 8 * i) % 128), device_id_type=pl.DeviceIdType.MESH)

    @pl.loop(1, 8, unroll=True)
    def _(i):
        pl.semaphore_signal(barrier, inc=1, device_id=device((me + i) % 128), device_id_type=pl.DeviceIdType.MESH)
        pl.semaphore_signal(barrier, inc=1, device_id=device((me + 128 - i) % 128), device_id_type=pl.DeviceIdType.MESH)

    def pad(held, given):
        held[...] = jnp.full((16, 256), -1, I32)
        held[:, :189] = given[...]

    small[0].wait()
    small[1].wait()
    pad(pfar, pfar_in)
    pad(ptype, ptype_in)

    kinds = rows_of((TPAD, 256))
    prow = rows_of((256, 256))
    parent = (prow // 16) * 16 + (prow % 8) * 2 + (prow // 8) % 2

    @pl.loop(0, 16, unroll=True)
    def _(g):
        a = onehot(pfar[pl.ds(g, 1), :] == parent)
        b = onehot(ptype[pl.ds(g, 1), :] == kinds)
        n_hi[pl.ds(pl.multiple_of(g * 256, 256), 256), :] = nt(a, b).astype(BF16)

    small[2].wait()
    dens_f[...] = dens[...].astype(F32)
    d_re = dens_f[pl.ds(0, 16, stride=2), :]
    d_im = dens_f[pl.ds(1, 16, stride=2), :]
    d_all = jnp.concatenate([d_re, d_im], 0)
    own = rows_of((32, 128)) % 16
    acc = jnp.zeros((32, 1024), F32)
    rad_copy.wait()
    for i in range(8):
        lhs = jnp.concatenate(
            [jnp.where(own == 2 * i + h, d_all, 0.0).astype(BF16) for h in range(2)], 1
        )
        acc = acc + nn(lhs, rad_v[i * 256 : (i + 1) * 256])
    tile_copy.start()
    rec_copy.start()
    def send(src, dst, ss, rs, pos):
        return pltpu.make_async_remote_copy(
            src_ref=src, dst_ref=dst, send_sem=ss, recv_sem=rs, device_id=device(pos), device_id_type=pl.DeviceIdType.MESH
        )

    pat = jnp.concatenate([acc[:16, :512] - acc[16:, 512:], acc[:16, 512:] + acc[16:, :512]], 0).astype(BF16)
    pat_f = pat.astype(F32)
    for m in range(2):
        for b in range(4):
            patf[pl.ds(m * 4 + b, 16, stride=8), :] = pat_f[m * 16 : (m + 1) * 16, b * 128 : (b + 1) * 128]
    pat3[...] = patf[...].reshape(16, 8, 128)
    small[3].wait()
    for m in range(2):
        for b in range(16):
            shifts[m, :, b * 128 : (b + 1) * 128] = shift_rows[pl.ds(b * 2 + m, 8, stride=32), :]

    def wait_for(ref, copies, sem):
        part = ref.at[pl.ds(0, copies)]
        pltpu.make_async_copy(part, part, sem).wait()

    def fill(dst, j, receiver):
        for half in range(2):
            parts = []
            for k in range(2):
                box = jnp.minimum(sb[half * 2 + k, receiver], 15)
                parts.append(pat3[box])
            dst[j, pl.ds(half * 16, 16), :] = jnp.concatenate(parts, 0).astype(BF16)

    def near_send(j):
        return send(leaf_msg.at[j], leaf_in.at[16 - j], leaf_s, leaf_r, (me + j + 120) % 128)

    def jump_send(i):
        return send(
            leaf_msg.at[17 + i], leaf_in.at[21 - i], leaf_s, leaf_r, (me + JUMPS[i]) % 128
        )

    int_copy.wait()
    up = nn(pat, int_v[...])
    s_re = shifts[0]
    s_im = shifts[1]
    for p in range(2):
        re = up[p * 8 : p * 8 + 8]
        im = up[16 + p * 8 : 24 + p * 8]
        vals = (
            jnp.sum(re * s_re - im * s_im, 0, keepdims=True),
            jnp.sum(re * s_im + im * s_re, 0, keepdims=True),
        )
        for m in range(2):
            for c in range(8):
                for h in range(2):
                    b = c * 2 + h
                    hi_scr[c, pl.ds(m * 4 + h * 2 + p, 1), :] = vals[m][:, b * 128 : (b + 1) * 128]
    one_msg[...] = hi_scr[...].astype(BF16)

    def one_send(i):
        peer = (zc + i) % 8
        return send(one_msg.at[peer], one_in.at[zc], one_s, one_r, yx * 8 + peer)

    for c in small[4:]:
        c.wait()
    nidx[...] = jnp.full((8, 128), -1, I32)
    for g in range(16):
        at = (g % 4) * 32
        nidx[g // 4 : g // 4 + 1, at : at + 27] = near_src[g : g + 1, :]
        nidx[4 + g // 4 : 5 + g // 4, at : at + 27] = near_tile[g : g + 1, :]
    pad(dps, dps_in)
    pad(ftype, ftype_in)
    hi_copy.wait()

    @pl.loop(0, 4)
    def _(i):
        hi_f[pl.ds(pl.multiple_of(i * 1264, 16), 1264), :] = hi_v[pl.ds(i * 79, 79)].astype(F32).reshape(1264, 128)

    hi_f[5056:, :] = jnp.zeros((1088, 128), F32)
    for r in range(4):
        at = (r % 2) * 256 + (r // 2) * 128
        thi[:, at : at + 128] = hi_f[pl.ds((zc % 4) * 4 + r, TPAD, stride=16), :].astype(BF16)

    lo_copy.wait()
    hi_f[:2528, :] = lo_v[...].astype(F32)
    hi_f[2528:3072, :] = jnp.zeros((544, 128), F32)
    for r in range(8):
        at = (r % 2) * 512 + (r // 2) * 128
        tlo[:, at : at + 128] = hi_f[pl.ds(r, TPAD, stride=8), :].astype(BF16)

    row = rows_of((96, 256))
    slot = row // 4
    delta = jnp.where(
        slot <= 16,
        slot - 8,
        jnp.where(slot == 17, 16, jnp.where(slot == 18, 32, jnp.where(slot == 19, 64, jnp.where(slot == 20, 96, 112)))),
    )
    expect = jnp.where(row < 88, ((me + delta + 128) % 128) * 4 + row % 4, -2)

    @pl.loop(0, 16, unroll=True)
    def _(g):
        a = onehot(dps[pl.ds(g, 1), :] == expect)
        b = onehot(ftype[pl.ds(g, 1), :] == kinds)
        n_lo[pl.ds(pl.multiple_of(g * 96, 32), 96), :] = nt(a, b).astype(BF16)

    tile_rows = me * 224 + rows_of((224, 128))
    live = jnp.concatenate([onehot(nidx[pl.ds(4 + r, 1), :] == tile_rows) for r in range(4)], 1)
    box_rows = (me - 1) * 16 + rows_of((48, 128))
    source = jnp.concatenate([onehot(nidx[pl.ds(r, 1), :] == box_rows) for r in range(4)], 1)
    owner = jnp.concatenate(
        [onehot(rows_of((16, 128)) == 4 * r + lanes_of((16, 128)) // 32) for r in range(4)], 1
    )
    own_tile = nt(owner, live).astype(BF16)
    select = nt(live, source).astype(BF16)

    pl.semaphore_wait(barrier, 29)

    @pl.loop(1, 8)
    def _(i):
        one_send(i).start()

    one_in[zc] = one_msg[zc]

    up_copy = send(dens, window.at[0], win_s, win_r, (me + 1) % 128)
    low_copy = send(dens, window.at[2], win_s, win_r, (me + 127) % 128)
    up_copy.start()
    low_copy.start()
    window[1] = dens[...]

    @pl.loop(0, 8)
    def _(j):
        fill(leaf_msg, j, (me + j + 120) % 128)
        near_send(j).start()

    @pl.loop(9, 17)
    def _(j):
        fill(leaf_msg, j, (me + j + 120) % 128)
        near_send(j).start()

    for i in range(5):
        fill(leaf_msg, 17 + i, (me + JUMPS[i]) % 128)
        jump_send(i).start()
    fill(leaf_in, 8, me)

    w_lo[...] = nn(n_lo[...], tlo[...])

    wait_for(one_in, 7, one_r)

    one_f[...] = one_in[...].astype(F32).reshape(64, 128)
    for m in range(4):
        two_msg[m] = jnp.concatenate(
            [one_f[pl.ds(m * 2 + p, 8, stride=8), :] for p in range(2)], 0
        ).astype(BF16)

    def two_send(i):
        peer = (yx + i) % 16
        return send(two_msg, two_in.at[yx], two_s, two_r, peer * 8 + zc)

    @pl.loop(1, 16)
    def _(i):
        two_send(i).start()

    two_in[yx] = two_msg[...]

    w_hi[...] = nn(n_hi[...], thi[...])

    wait_for(window, 2, win_r)
    win_f[...] = window[...].astype(F32).reshape(96, 128)
    x_re = win_f[pl.ds(0, 48, stride=2), :]
    x_im = win_f[pl.ds(1, 48, stride=2), :]
    values = jnp.concatenate([x_re, -x_im, x_im, x_re], 1).astype(BF16)
    picked[...] = nn(select, values).astype(BF16)

    tile_copy.wait()

    def near_group(grp):
        base = grp * GROUP
        x = picked[base : base + GROUP, :]
        lhs = jnp.concatenate([x[:, :256], x[:, 256:]], 0)
        local = rows_of((2 * GROUP, 128)) % GROUP
        total = jnp.zeros((2 * GROUP, 128), F32)
        for q in range(GROUP // 2):
            pair = []
            for u in range(2):
                t = base + 2 * q + u
                pair.append(jnp.concatenate([tile_v[t, 0], tile_v[t, 1]], 1))
            res = nt(lhs, jnp.concatenate(pair, 0))
            for u in range(2):
                total = total + jnp.where(local == 2 * q + u, res[:, u * 128 : (u + 1) * 128], 0.0)
        contrib[base : base + GROUP, :] = jnp.concatenate([total[:GROUP], total[GROUP:]], 1)

    for grp in range(12):
        near_group(grp)

    wait_for(two_in, 15, two_r)

    for m in range(4):
        for i in range(16):
            hi_p[m, i * 16 : (i + 1) * 16, :] = two_in[i, m].astype(F32)

    for c in range(8):
        for p in range(2):
            base = (c * 2 + p) * 256
            for h in range(2):
                wr = w_hi[base : base + 256, h * 128 : (h + 1) * 128]
                wi = w_hi[base : base + 256, 256 + h * 128 : 256 + (h + 1) * 128]
                pr = hi_p[h]
                pi = hi_p[2 + h]
                ret_msg[c, pl.ds(h * 2 + p, 1), :] = jnp.sum(wr * pr - wi * pi, 0, keepdims=True)
                ret_msg[c, pl.ds(4 + h * 2 + p, 1), :] = jnp.sum(wr * pi + wi * pr, 0, keepdims=True)

    def ret_send(i):
        peer = (zc + i) % 8
        return send(ret_msg.at[peer], ret_in.at[zc], ret_s, ret_r, yx * 8 + peer)

    @pl.loop(1, 8)
    def _(i):
        ret_send(i).start()

    ret_in[zc] = ret_msg[zc]

    wait_for(leaf_in, 21, leaf_r)
    p_lo[...] = leaf_in[...].astype(F32).reshape(704, 128)

    def leaf_sum(g):
        base = g * 96
        reals, imags = [], []
        for b in range(4):
            wr = w_lo[base : base + 88, b * 128 : (b + 1) * 128]
            wi = w_lo[base : base + 88, 512 + b * 128 : 512 + (b + 1) * 128]
            pr = p_lo[pl.ds(b, 88, stride=8), :]
            pi = p_lo[pl.ds(4 + b, 88, stride=8), :]
            reals.append(jnp.sum(wr * pr - wi * pi, 0, keepdims=True))
            imags.append(jnp.sum(wr * pi + wi * pr, 0, keepdims=True))
        inc_lo[g * 8 : g * 8 + 8, :] = jnp.concatenate(reals + imags, 0)

    for grp in range(12, groups):
        near_group(grp)

    for g in range(16):
        leaf_sum(g)

    whole = contrib[...]
    high = whole.astype(BF16)
    near = nn(own_tile, high) + nn(own_tile, (whole - high.astype(F32)).astype(BF16))

    wait_for(window, 2, win_s)
    wait_for(one_in, 7, one_s)
    wait_for(two_in, 15, two_s)
    wait_for(leaf_in, 21, leaf_s)
    wait_for(ret_in, 7, ret_s)

    wait_for(ret_in, 7, ret_r)

    for c in range(8):
        for h in range(2):
            b = c * 2 + h
            sr = shifts[0, :, b * 128 : (b + 1) * 128]
            si = shifts[1, :, b * 128 : (b + 1) * 128]
            parts = ([], [])
            for p in range(2):
                ir = ret_in[c, pl.ds(h * 2 + p, 1), :]
                ii = ret_in[c, pl.ds(4 + h * 2 + p, 1), :]
                parts[0].append(sr * ir + si * ii)
                parts[1].append(sr * ii - si * ir)
            for m in range(2):
                down[m * 16 : (m + 1) * 16, b * 128 : (b + 1) * 128] = jnp.concatenate(parts[m], 0).astype(BF16)
    direct = jnp.concatenate(
        [
            jnp.concatenate([inc_lo[pl.ds(m * 4 + b, 16, stride=8), :] for b in range(4)], 1)
            for m in range(2)
        ],
        0,
    )
    incoming = (direct + nt(down[...], int_v[...])).astype(BF16)
    in_re = incoming[:16]
    in_im = incoming[16:]
    lhs = jnp.concatenate([jnp.concatenate([in_re, -in_im], 1), jnp.concatenate([in_im, in_re], 1)], 0)
    far = jnp.zeros((32, 128), F32)
    rec_copy.wait()
    for i in range(8):
        res = nt(lhs, rec_v[i * 256 : (i + 1) * 256])
        for u in range(2):
            far = far + jnp.where(own == 2 * i + u, res[:, u * 128 : (u + 1) * 128], 0.0)
    out[pl.ds(0, 16, stride=2), :] = near[:, :128] + far[:16]
    out[pl.ds(1, 16, stride=2), :] = near[:, 128:] + far[16:]


def on_device(
    density, radiate, receive, near_tiles, near_src, near_tile, send_box, distant_pattern_slot, far_type,
    trans_lo, interp_matrix, shifts, par_far, par_type, trans_hi,
):
    types = trans_lo.shape[0]
    lo_rows = trans_lo.reshape(types, 2, 4, 128).transpose(0, 2, 1, 3).reshape(types * 8, 128)
    hi_rows = trans_hi.reshape(types, 2, 16, 128).transpose(0, 2, 1, 3).reshape(types, 32, 128)
    shift_rows = shifts.reshape(8, 2, 16, 128).transpose(0, 2, 1, 3).reshape(256, 128)

    vm = pl.BlockSpec(memory_space=pltpu.VMEM)
    anyspace = pl.BlockSpec(memory_space=pl.ANY)
    dma = pltpu.SemaphoreType.DMA
    res = pl.pallas_call(
        kernel,
        name="mlfmm",
        out_shape=pltpu.VMEM((32, 128), F32),
        in_specs=[anyspace, pl.BlockSpec(memory_space=pltpu.SMEM)] + [anyspace] * 13,
        out_specs=vm,
        scratch_shapes=[
            pltpu.VMEM((32, 128), BF16),
            pltpu.VMEM((16, 27), I32),
            pltpu.VMEM((16, 27), I32),
            pltpu.VMEM((16, 189), I32),
            pltpu.VMEM((16, 189), I32),
            pltpu.VMEM((16, 189), I32),
            pltpu.VMEM((16, 189), I32),
            pltpu.VMEM((256, 128), F32),
            dma((8,)),
            pltpu.VMEM((32, 128), F32),
            pltpu.VMEM((96, 128), F32),
            pltpu.VMEM((8, 128), I32),
            pltpu.VMEM((16, 256), I32),
            pltpu.VMEM((16, 256), I32),
            pltpu.VMEM((16, 256), I32),
            pltpu.VMEM((16, 256), I32),
            pltpu.VMEM((2, 8, 2048), F32),
            pltpu.VMEM((2528, 128), BF16),
            pltpu.VMEM((316, 16, 128), BF16),
            pltpu.VMEM((TPAD * 16, 128), F32),
            pltpu.VMEM((TPAD, 1024), BF16),
            pltpu.VMEM((TPAD, 512), BF16),
            pltpu.VMEM((16, 8, 128), F32),
            dma,
            dma,
            pltpu.VMEM((2048, 1024), BF16),
            pltpu.VMEM((2048, 1024), BF16),
            pltpu.VMEM((224, 2, 128, 128), BF16),
            pltpu.VMEM((512, 2048), BF16),
            pltpu.VMEM((3, 32, 128), BF16),
            pltpu.VMEM((128, 128), F32),
            pltpu.VMEM((22, 32, 128), BF16),
            pltpu.VMEM((22, 32, 128), BF16),
            pltpu.VMEM((8, 8, 128), F32),
            pltpu.VMEM((8, 8, 128), BF16),
            pltpu.VMEM((8, 8, 128), BF16),
            pltpu.VMEM((64, 128), F32),
            pltpu.VMEM((4, 16, 128), BF16),
            pltpu.VMEM((16, 4, 16, 128), BF16),
            pltpu.VMEM((4, 256, 128), F32),
            pltpu.VMEM((8, 8, 128), F32),
            pltpu.VMEM((8, 8, 128), F32),
            pltpu.VMEM((32, 2048), BF16),
            pltpu.VMEM((1536, TPAD), BF16),
            pltpu.VMEM((1536, 1024), F32),
            pltpu.VMEM((704, 128), F32),
            pltpu.VMEM((4096, TPAD), BF16),
            pltpu.VMEM((4096, 512), F32),
            pltpu.VMEM((128, 128), F32),
            pltpu.VMEM((224, 256), F32),
            pltpu.VMEM((224, 512), BF16),
            dma,
            dma,
            dma,
            dma,
            dma,
            dma,
            dma,
            dma,
            dma,
            dma,
            dma,
            dma,
            dma,
            dma,
            dma,
        ],
        compiler_params=pltpu.CompilerParams(
            collective_id=0, has_side_effects=True, vmem_limit_bytes=59 * 1024 * 1024
        ),
    )(
        density.reshape(32, 128), send_box.reshape(128, 4).transpose(1, 0), near_src, near_tile,
        distant_pattern_slot, far_type, par_far, par_type, shift_rows,
        radiate.reshape(2048, 1024), receive.reshape(2048, 1024), near_tiles, interp_matrix, lo_rows, hi_rows,
    )
    return (res + 0.5 * density.reshape(32, 128).astype(F32)).reshape(16, 2, 128)


def solution(mesh):
    both = ("box", "samp")
    return jax.shard_map(
        on_device,
        mesh=mesh,
        in_specs=(
            P(both, None, None), P(both, None, None), P(both, None, None), P(both, None, None, None),
            P(both, None), P(both, None), P(both, None, None), P(both, None), P(both, None),
            P(), P(), P(), P("box", None), P("box", None), P(),
        ),
        out_specs=P(both, None, None),
        check_vma=False,
    )
```

```python
import functools

import jax
import jax.numpy as jnp
from jax import lax
from jax.experimental import pallas as pl
from jax.experimental.pallas import tpu as pltpu
from jax.sharding import PartitionSpec as P

F32 = jnp.float32
BF16 = jnp.bfloat16
I32 = jnp.int32
JUMPS = (16, 32, 64, 96, 112)
TPAD = 320
GROUP = 16


def nn(a, b):
    return lax.dot_general(a, b, (((1,), (0,)), ((), ())), preferred_element_type=F32)


def nt(a, b):
    return lax.dot_general(a, b, (((1,), (1,)), ((), ())), preferred_element_type=F32)


def rows_of(shape):
    return lax.broadcasted_iota(I32, shape, 0)


def lanes_of(shape):
    return lax.broadcasted_iota(I32, shape, 1)


def onehot(mask):
    return jnp.where(mask, 1.0, 0.0).astype(BF16)


def device(pos):
    return (pos // 32, pos % 32)


def kernel(
    dens_h, sb_h, near_src_h, near_tile_h, dps_h, ftype_h, pfar_h, ptype_h, shift_h,
    radiate, receive, tiles, interp, lo_rows, hi_rows,
    out,
    sb, sb_sem, dens, near_src, near_tile, dps_in, ftype_in, pfar_in, ptype_in, shift_rows, small_sem,
    dens_f, win_f, nidx, dps, ftype, pfar, ptype, shifts, lo_v, hi_v, hi_f, tlo, thi, pat3, lo_sem, hi_sem,
    rad_v, rec_v, tile_v, int_v, window, patf, leaf_msg, leaf_in, hi_scr, one_msg, one_in, one_f,
    two_msg, two_in, hi_p, ret_msg, ret_in, down, n_lo, w_lo, p_lo, n_hi, w_hi, inc_lo, contrib, picked,
    rad_sem, rec_sem, tile_sem, int_sem, loc_sem,
    win_s, win_r, leaf_s, leaf_r, one_s, one_r, two_s, two_r, ret_s, ret_r,
):
    y = lax.axis_index("box")
    s = lax.axis_index("samp")
    me = y * 32 + s
    zc = s % 8
    yx = y * 4 + s // 8

    rad_copy = pltpu.make_async_copy(radiate, rad_v, rad_sem)
    rec_copy = pltpu.make_async_copy(receive, rec_v, rec_sem)
    tile_copy = pltpu.make_async_copy(tiles, tile_v, tile_sem)
    int_copy = pltpu.make_async_copy(interp, int_v, int_sem)
    groups = tiles.shape[0] // GROUP

    lo_copy = pltpu.make_async_copy(lo_rows, lo_v, lo_sem)
    hi_copy = pltpu.make_async_copy(hi_rows.at[:, pl.ds((zc // 4) * 16, 16), :], hi_v, hi_sem)

    column = s // 8
    part = pl.ds(pl.multiple_of(column * 16, 16), 16)
    small = [
        pltpu.make_async_copy(a, b, small_sem.at[i])
        for i, (a, b) in enumerate(
            (
                (pfar_h.at[part], pfar_in), (ptype_h.at[part], ptype_in), (dens_h, dens), (shift_h, shift_rows),
                (near_src_h, near_src), (near_tile_h, near_tile), (dps_h, dps_in), (ftype_h, ftype_in),
            )
        )
    ]
    for c in small[:3]:
        c.start()
    rad_copy.start()
    int_copy.start()
    box_copy = pltpu.make_async_copy(sb_h, sb, sb_sem)
    box_copy.start()
    for c in small[3:]:
        c.start()
    lo_copy.start()
    hi_copy.start()

    barrier = pltpu.get_barrier_semaphore()

    @pl.loop(1, 16, unroll=True)
    def _(i):
        pl.semaphore_signal(barrier, inc=1, device_id=device((me + 8 * i) % 128), device_id_type=pl.DeviceIdType.MESH)

    @pl.loop(1, 8, unroll=True)
    def _(i):
        pl.semaphore_signal(barrier, inc=1, device_id=device((me + i) % 128), device_id_type=pl.DeviceIdType.MESH)
        pl.semaphore_signal(barrier, inc=1, device_id=device((me + 128 - i) % 128), device_id_type=pl.DeviceIdType.MESH)

    def pad(held, given):
        held[...] = jnp.full((16, 256), -1, I32)
        held[:, :189] = given[...]

    small[0].wait()
    small[1].wait()
    pad(pfar, pfar_in)
    pad(ptype, ptype_in)

    kinds = rows_of((TPAD, 256))
    prow = rows_of((256, 256))
    parent = (prow // 16) * 16 + (prow % 8) * 2 + (prow // 8) % 2

    @pl.loop(0, 16, unroll=True)
    def _(g):
        a = onehot(pfar[pl.ds(g, 1), :] == parent)
        b = onehot(ptype[pl.ds(g, 1), :] == kinds)
        n_hi[pl.ds(pl.multiple_of(g * 256, 256), 256), :] = nt(a, b).astype(BF16)

    small[2].wait()
    dens_f[...] = dens[...].astype(F32)
    d_re = dens_f[pl.ds(0, 16, stride=2), :]
    d_im = dens_f[pl.ds(1, 16, stride=2), :]
    d_all = jnp.concatenate([d_re, d_im], 0)
    own = rows_of((32, 128)) % 16
    acc = jnp.zeros((32, 1024), F32)
    rad_copy.wait()
    for i in range(8):
        lhs = jnp.concatenate(
            [jnp.where(own == 2 * i + h, d_all, 0.0).astype(BF16) for h in range(2)], 1
        )
        acc = acc + nn(lhs, rad_v[i * 256 : (i + 1) * 256])
    tile_copy.start()
    rec_copy.start()
    def send(src, dst, ss, rs, pos):
        return pltpu.make_async_remote_copy(
            src_ref=src, dst_ref=dst, send_sem=ss, recv_sem=rs, device_id=device(pos), device_id_type=pl.DeviceIdType.MESH
        )

    pat = jnp.concatenate([acc[:16, :512] - acc[16:, 512:], acc[:16, 512:] + acc[16:, :512]], 0).astype(BF16)
    pat_f = pat.astype(F32)
    for m in range(2):
        for b in range(4):
            patf[pl.ds(m * 4 + b, 16, stride=8), :] = pat_f[m * 16 : (m + 1) * 16, b * 128 : (b + 1) * 128]
    box_copy.wait()
    pat3[...] = patf[...].reshape(16, 8, 128)
    small[3].wait()
    for m in range(2):
        for b in range(16):
            shifts[m, :, b * 128 : (b + 1) * 128] = shift_rows[pl.ds(b * 2 + m, 8, stride=32), :]

    def wait_for(ref, copies, sem):
        part = ref.at[pl.ds(0, copies)]
        pltpu.make_async_copy(part, part, sem).wait()

    def fill(dst, j, receiver):
        for half in range(2):
            parts = []
            for k in range(2):
                box = jnp.minimum(sb[half * 2 + k, receiver], 15)
                parts.append(pat3[box])
            dst[j, pl.ds(half * 16, 16), :] = jnp.concatenate(parts, 0).astype(BF16)

    def near_send(j):
        return send(leaf_msg.at[j], leaf_in.at[16 - j], leaf_s, leaf_r, (me + j + 120) % 128)

    def jump_send(i):
        return send(
            leaf_msg.at[17 + i], leaf_in.at[21 - i], leaf_s, leaf_r, (me + JUMPS[i]) % 128
        )

    int_copy.wait()
    up = nn(pat, int_v[...])
    s_re = shifts[0]
    s_im = shifts[1]
    for p in range(2):
        re = up[p * 8 : p * 8 + 8]
        im = up[16 + p * 8 : 24 + p * 8]
        vals = (
            jnp.sum(re * s_re - im * s_im, 0, keepdims=True),
            jnp.sum(re * s_im + im * s_re, 0, keepdims=True),
        )
        for m in range(2):
            for c in range(8):
                for h in range(2):
                    b = c * 2 + h
                    hi_scr[c, pl.ds(m * 4 + h * 2 + p, 1), :] = vals[m][:, b * 128 : (b + 1) * 128]
    one_msg[...] = hi_scr[...].astype(BF16)

    def one_send(i):
        peer = (zc + i) % 8
        return send(one_msg.at[peer], one_in.at[zc], one_s, one_r, yx * 8 + peer)

    for c in small[4:]:
        c.wait()
    nidx[...] = jnp.full((8, 128), -1, I32)
    for g in range(16):
        at = (g % 4) * 32
        nidx[g // 4 : g // 4 + 1, at : at + 27] = near_src[g : g + 1, :]
        nidx[4 + g // 4 : 5 + g // 4, at : at + 27] = near_tile[g : g + 1, :]
    pad(dps, dps_in)
    pad(ftype, ftype_in)
    hi_copy.wait()

    @pl.loop(0, 4)
    def _(i):
        hi_f[pl.ds(pl.multiple_of(i * 1264, 16), 1264), :] = hi_v[pl.ds(i * 79, 79)].astype(F32).reshape(1264, 128)

    hi_f[5056:, :] = jnp.zeros((64, 128), F32)
    for r in range(4):
        at = (r % 2) * 256 + (r // 2) * 128
        thi[:, at : at + 128] = hi_f[pl.ds((zc % 4) * 4 + r, TPAD, stride=16), :].astype(BF16)

    lo_copy.wait()
    hi_f[:2528, :] = lo_v[...].astype(F32)
    hi_f[2528:2560, :] = jnp.zeros((32, 128), F32)
    for r in range(8):
        at = (r % 2) * 512 + (r // 2) * 128
        tlo[:, at : at + 128] = hi_f[pl.ds(r, TPAD, stride=8), :].astype(BF16)

    row = rows_of((96, 256))
    slot = row // 4
    delta = jnp.where(
        slot <= 16,
        slot - 8,
        jnp.where(slot == 17, 16, jnp.where(slot == 18, 32, jnp.where(slot == 19, 64, jnp.where(slot == 20, 96, 112)))),
    )
    expect = jnp.where(row < 88, ((me + delta + 128) % 128) * 4 + row % 4, -2)

    @pl.loop(0, 16, unroll=True)
    def _(g):
        a = onehot(dps[pl.ds(g, 1), :] == expect)
        b = onehot(ftype[pl.ds(g, 1), :] == kinds)
        n_lo[pl.ds(pl.multiple_of(g * 96, 32), 96), :] = nt(a, b).astype(BF16)

    tile_rows = me * 224 + rows_of((224, 128))
    live = jnp.concatenate([onehot(nidx[pl.ds(4 + r, 1), :] == tile_rows) for r in range(4)], 1)
    box_rows = (me - 1) * 16 + rows_of((48, 128))
    source = jnp.concatenate([onehot(nidx[pl.ds(r, 1), :] == box_rows) for r in range(4)], 1)
    owner = jnp.concatenate(
        [onehot(rows_of((16, 128)) == 4 * r + lanes_of((16, 128)) // 32) for r in range(4)], 1
    )
    own_tile = nt(owner, live).astype(BF16)
    select = nt(live, source).astype(BF16)

    pl.semaphore_wait(barrier, 29)

    @pl.loop(1, 8)
    def _(i):
        one_send(i).start()

    one_in[zc] = one_msg[zc]

    up_copy = send(dens, window.at[0], win_s, win_r, (me + 1) % 128)
    low_copy = send(dens, window.at[2], win_s, win_r, (me + 127) % 128)
    up_copy.start()
    low_copy.start()
    window[1] = dens[...]

    w_lo[...] = nn(n_lo[...], tlo[...])

    wait_for(one_in, 7, one_r)

    one_f[...] = one_in[...].astype(F32).reshape(64, 128)
    for m in range(4):
        two_msg[m] = jnp.concatenate(
            [one_f[pl.ds(m * 2 + p, 8, stride=8), :] for p in range(2)], 0
        ).astype(BF16)

    def two_send(i):
        peer = (yx + i) % 16
        return send(two_msg, two_in.at[yx], two_s, two_r, peer * 8 + zc)

    @pl.loop(1, 16)
    def _(i):
        two_send(i).start()

    two_in[yx] = two_msg[...]

    @pl.loop(0, 8)
    def _(j):
        fill(leaf_msg, j, (me + j + 120) % 128)
        near_send(j).start()

    @pl.loop(9, 17)
    def _(j):
        fill(leaf_msg, j, (me + j + 120) % 128)
        near_send(j).start()

    for i in range(5):
        fill(leaf_msg, 17 + i, (me + JUMPS[i]) % 128)
        jump_send(i).start()
    fill(leaf_in, 8, me)

    w_hi[...] = nn(n_hi[...], thi[...])

    wait_for(window, 2, win_r)
    win_f[...] = window[...].astype(F32).reshape(96, 128)
    x_re = win_f[pl.ds(0, 48, stride=2), :]
    x_im = win_f[pl.ds(1, 48, stride=2), :]
    values = jnp.concatenate([x_re, -x_im, x_im, x_re], 1).astype(BF16)
    picked[...] = nn(select, values).astype(BF16)

    tile_copy.wait()

    def near_group(grp):
        base = grp * GROUP
        x = picked[base : base + GROUP, :]
        lhs = jnp.concatenate([x[:, :256], x[:, 256:]], 0)
        local = rows_of((2 * GROUP, 128)) % GROUP
        total = jnp.zeros((2 * GROUP, 128), F32)
        for q in range(GROUP // 2):
            pair = []
            for u in range(2):
                t = base + 2 * q + u
                pair.append(jnp.concatenate([tile_v[t, 0], tile_v[t, 1]], 1))
            res = nt(lhs, jnp.concatenate(pair, 0))
            for u in range(2):
                total = total + jnp.where(local == 2 * q + u, res[:, u * 128 : (u + 1) * 128], 0.0)
        contrib[base : base + GROUP, :] = jnp.concatenate([total[:GROUP], total[GROUP:]], 1)

    for grp in range(12):
        near_group(grp)

    wait_for(two_in, 15, two_r)

    for m in range(4):
        for i in range(16):
            hi_p[m, i * 16 : (i + 1) * 16, :] = two_in[i, m].astype(F32)

    for c in range(8):
        for p in range(2):
            base = (c * 2 + p) * 256
            for h in range(2):
                wr = w_hi[base : base + 256, h * 128 : (h + 1) * 128]
                wi = w_hi[base : base + 256, 256 + h * 128 : 256 + (h + 1) * 128]
                pr = hi_p[h]
                pi = hi_p[2 + h]
                ret_msg[c, pl.ds(h * 2 + p, 1), :] = jnp.sum(wr * pr - wi * pi, 0, keepdims=True)
                ret_msg[c, pl.ds(4 + h * 2 + p, 1), :] = jnp.sum(wr * pi + wi * pr, 0, keepdims=True)

    def ret_send(i):
        peer = (zc + i) % 8
        return send(ret_msg.at[peer], ret_in.at[zc], ret_s, ret_r, yx * 8 + peer)

    @pl.loop(1, 8)
    def _(i):
        ret_send(i).start()

    ret_in[zc] = ret_msg[zc]

    wait_for(leaf_in, 21, leaf_r)
    p_lo[...] = leaf_in[...].astype(F32).reshape(704, 128)

    def leaf_sum(g):
        base = g * 96
        reals, imags = [], []
        for b in range(4):
            wr = w_lo[base : base + 88, b * 128 : (b + 1) * 128]
            wi = w_lo[base : base + 88, 512 + b * 128 : 512 + (b + 1) * 128]
            pr = p_lo[pl.ds(b, 88, stride=8), :]
            pi = p_lo[pl.ds(4 + b, 88, stride=8), :]
            reals.append(jnp.sum(wr * pr - wi * pi, 0, keepdims=True))
            imags.append(jnp.sum(wr * pi + wi * pr, 0, keepdims=True))
        inc_lo[g * 8 : g * 8 + 8, :] = jnp.concatenate(reals + imags, 0)

    for grp in range(12, groups):
        near_group(grp)

    for g in range(16):
        leaf_sum(g)

    whole = contrib[...]
    high = whole.astype(BF16)
    near = nn(own_tile, high) + nn(own_tile, (whole - high.astype(F32)).astype(BF16))

    wait_for(window, 2, win_s)
    wait_for(one_in, 7, one_s)
    wait_for(two_in, 15, two_s)
    wait_for(leaf_in, 21, leaf_s)
    wait_for(ret_in, 7, ret_s)

    wait_for(ret_in, 7, ret_r)

    for c in range(8):
        for h in range(2):
            b = c * 2 + h
            sr = shifts[0, :, b * 128 : (b + 1) * 128]
            si = shifts[1, :, b * 128 : (b + 1) * 128]
            parts = ([], [])
            for p in range(2):
                ir = ret_in[c, pl.ds(h * 2 + p, 1), :]
                ii = ret_in[c, pl.ds(4 + h * 2 + p, 1), :]
                parts[0].append(sr * ir + si * ii)
                parts[1].append(sr * ii - si * ir)
            for m in range(2):
                down[m * 16 : (m + 1) * 16, b * 128 : (b + 1) * 128] = jnp.concatenate(parts[m], 0).astype(BF16)
    direct = jnp.concatenate(
        [
            jnp.concatenate([inc_lo[pl.ds(m * 4 + b, 16, stride=8), :] for b in range(4)], 1)
            for m in range(2)
        ],
        0,
    )
    incoming = (direct + nt(down[...], int_v[...])).astype(BF16)
    in_re = incoming[:16]
    in_im = incoming[16:]
    lhs = jnp.concatenate([jnp.concatenate([in_re, -in_im], 1), jnp.concatenate([in_im, in_re], 1)], 0)
    far = jnp.zeros((32, 128), F32)
    rec_copy.wait()
    for i in range(8):
        res = nt(lhs, rec_v[i * 256 : (i + 1) * 256])
        for u in range(2):
            far = far + jnp.where(own == 2 * i + u, res[:, u * 128 : (u + 1) * 128], 0.0)
    out[pl.ds(0, 16, stride=2), :] = near[:, :128] + far[:16]
    out[pl.ds(1, 16, stride=2), :] = near[:, 128:] + far[16:]


def on_device(
    density, radiate, receive, near_tiles, near_src, near_tile, send_box, distant_pattern_slot, far_type,
    trans_lo, interp_matrix, shifts, par_far, par_type, trans_hi,
):
    types = trans_lo.shape[0]
    lo_rows = trans_lo.reshape(types, 2, 4, 128).transpose(0, 2, 1, 3).reshape(types * 8, 128)
    hi_rows = trans_hi.reshape(types, 2, 16, 128).transpose(0, 2, 1, 3).reshape(types, 32, 128)
    shift_rows = shifts.reshape(8, 2, 16, 128).transpose(0, 2, 1, 3).reshape(256, 128)

    vm = pl.BlockSpec(memory_space=pltpu.VMEM)
    anyspace = pl.BlockSpec(memory_space=pl.ANY)
    dma = pltpu.SemaphoreType.DMA
    res = pl.pallas_call(
        kernel,
        name="mlfmm",
        out_shape=pltpu.VMEM((32, 128), F32),
        in_specs=[anyspace] * 15,
        out_specs=vm,
        scratch_shapes=[
            pltpu.SMEM((4, 128), I32),
            dma,
            pltpu.VMEM((32, 128), BF16),
            pltpu.VMEM((16, 27), I32),
            pltpu.VMEM((16, 27), I32),
            pltpu.VMEM((16, 189), I32),
            pltpu.VMEM((16, 189), I32),
            pltpu.VMEM((16, 189), I32),
            pltpu.VMEM((16, 189), I32),
            pltpu.VMEM((256, 128), F32),
            dma((8,)),
            pltpu.VMEM((32, 128), F32),
            pltpu.VMEM((96, 128), F32),
            pltpu.VMEM((8, 128), I32),
            pltpu.VMEM((16, 256), I32),
            pltpu.VMEM((16, 256), I32),
            pltpu.VMEM((16, 256), I32),
            pltpu.VMEM((16, 256), I32),
            pltpu.VMEM((2, 8, 2048), F32),
            pltpu.VMEM((2528, 128), BF16),
            pltpu.VMEM((316, 16, 128), BF16),
            pltpu.VMEM((TPAD * 16, 128), F32),
            pltpu.VMEM((TPAD, 1024), BF16),
            pltpu.VMEM((TPAD, 512), BF16),
            pltpu.VMEM((16, 8, 128), F32),
            dma,
            dma,
            pltpu.VMEM((2048, 1024), BF16),
            pltpu.VMEM((2048, 1024), BF16),
            pltpu.VMEM((224, 2, 128, 128), BF16),
            pltpu.VMEM((512, 2048), BF16),
            pltpu.VMEM((3, 32, 128), BF16),
            pltpu.VMEM((128, 128), F32),
            pltpu.VMEM((22, 32, 128), BF16),
            pltpu.VMEM((22, 32, 128), BF16),
            pltpu.VMEM((8, 8, 128), F32),
            pltpu.VMEM((8, 8, 128), BF16),
            pltpu.VMEM((8, 8, 128), BF16),
            pltpu.VMEM((64, 128), F32),
            pltpu.VMEM((4, 16, 128), BF16),
            pltpu.VMEM((16, 4, 16, 128), BF16),
            pltpu.VMEM((4, 256, 128), F32),
            pltpu.VMEM((8, 8, 128), F32),
            pltpu.VMEM((8, 8, 128), F32),
            pltpu.VMEM((32, 2048), BF16),
            pltpu.VMEM((1536, TPAD), BF16),
            pltpu.VMEM((1536, 1024), F32),
            pltpu.VMEM((704, 128), F32),
            pltpu.VMEM((4096, TPAD), BF16),
            pltpu.VMEM((4096, 512), F32),
            pltpu.VMEM((128, 128), F32),
            pltpu.VMEM((224, 256), F32),
            pltpu.VMEM((224, 512), BF16),
            dma,
            dma,
            dma,
            dma,
            dma,
            dma,
            dma,
            dma,
            dma,
            dma,
            dma,
            dma,
            dma,
            dma,
            dma,
        ],
        compiler_params=pltpu.CompilerParams(
            collective_id=0, has_side_effects=True, vmem_limit_bytes=59 * 1024 * 1024
        ),
    )(
        density.reshape(32, 128), send_box.reshape(128, 4).transpose(1, 0), near_src, near_tile,
        distant_pattern_slot, far_type, par_far, par_type, shift_rows,
        radiate.reshape(2048, 1024), receive.reshape(2048, 1024), near_tiles, interp_matrix, lo_rows, hi_rows,
    )
    return (res + 0.5 * density.reshape(32, 128).astype(F32)).reshape(16, 2, 128)


def solution(mesh):
    both = ("box", "samp")
    return jax.shard_map(
        on_device,
        mesh=mesh,
        in_specs=(
            P(both, None, None), P(both, None, None), P(both, None, None), P(both, None, None, None),
            P(both, None), P(both, None), P(both, None, None), P(both, None), P(both, None),
            P(), P(), P(), P("box", None), P("box", None), P(),
        ),
        out_specs=P(both, None, None),
        check_vma=False,
    )
```
